32 devices in a mesh: layer: 4 (over z), row: 2 (over x), col: 4 (over y, core).
Axes of the slice: x: 2, y: 2, z: 4, core: 2. Of those that a mesh axis runs over, the one named last changes fastest.
Arguments:
- cost_vector: float32 [8, 1024, 512], P('layer', 'row', 'col'), may hold values from -12 to 12
- metal_density: float32 [8, 1024, 512], P('layer', 'row', 'col'), may hold values from 0 to 0.5
- cap_class: int32 [8, 1024, 512], P('layer', 'row', 'col'), may hold values from 0 to 7
- blocked_mask: int32 [8, 1024, 512], P('layer', 'row', 'col'), may hold values 0 or 1
- fill_start: float32 [8, 1024, 512], P('layer', 'row', 'col'), may hold values from 0 to 1
- window_dual: float32 [8, 1024, 512], P('layer', 'row', 'col'), may hold values from -4 to 4
- layer_dual: float32 [8, 1024, 512], P('layer', 'row', 'col'), may hold values from -4 to 4
Outputs:
- fill_level: float32 [8, 1024, 512], P('layer', 'row', 'col')
- window_price: float32 [8, 1024, 512], P('layer', 'row', 'col')
- layer_price: float32 [8, 1024, 512], P('layer', 'row', 'col')
- primal_weight: float32 [], replicated
The draws below stay inside these ranges and needn't reach their ends.
All inputs are finite; a program needn't handle non-finite values. No bound on the sum of `blocked_mask` on one device may be relied on, other than what follows from the above.
Results may differ from the reference program's by a relative error of at most 0.00011.
Values sent between devices are 32-bit elements; how exact they have to be, the bound alone decides.
A program may use at most 64 MiB of HBM per device.

```python
import jax
import jax.numpy as jnp
from jax import lax

WIN = 50
CAP_LEVELS = 8
ITERS = 3
LAYERS = 8
ROWS = 1024
COLS = 512


def draw_cost_vector(key, part):
    first_key = jax.random.fold_in(key, 0)
    layer_pos = jnp.arange(LAYERS, dtype=jnp.float32)[:, None, None] / max(LAYERS - 1, 1)
    row_pos = jnp.arange(ROWS, dtype=jnp.float32)[None, :, None] / (ROWS - 1)
    col_pos = jnp.arange(COLS, dtype=jnp.float32)[None, None, :] / (COLS - 1)
    ramp_scale = 1.0 + 2.0 * (layer_pos + row_pos + col_pos) / 3.0
    base_draw = jax.random.normal(first_key, (LAYERS, ROWS, COLS), jnp.float32)
    return jnp.clip(base_draw * ramp_scale, -12.0, 12.0)


def touch_ends(array, own_key, least, largest):
    place = [jax.random.randint(jax.random.fold_in(own_key, axis), (), 0, length) for axis, length in enumerate(array.shape)]
    longest = array.shape.index(max(array.shape))
    beside = place[:longest] + [(place[longest] + 1) % array.shape[longest]] + place[longest + 1:]
    return array.at[tuple(place)].set(least).at[tuple(beside)].set(largest)


def block_scale(stream_key, shape, pieces, low, high):
    loudness = 1.0
    for axis_at, shards_of in pieces:
        draws = jax.random.uniform(jax.random.fold_in(jax.random.fold_in(stream_key, 6), axis_at), (shards_of,), jnp.float32, low / len(pieces), high / len(pieces))
        loudness = loudness * jnp.repeat(jnp.exp(draws), shape[axis_at] // shards_of).reshape((-1,) + (1,) * (len(shape) - 1 - axis_at))
    return loudness


def gaussian(key, dims, spread, reach, shards=(), held_as=jnp.bfloat16):
    result = spread * jax.random.normal(key, dims, jnp.float32)
    if shards:
        result = result * block_scale(key, dims, shards, -0.22, 0.18)
    return jnp.clip(result, -reach, reach).astype(held_as)


def setup_inputs(seed: int = 0) -> dict:
    key_of = jax.random.split(jax.random.key(seed), 8)
    return {
        "cost_vector": draw_cost_vector(jax.random.fold_in(key_of[7], 71), 0),
        "metal_density": jnp.clip(0.5 * jax.random.uniform(key_of[1], (LAYERS, ROWS, COLS), jnp.float32) ** block_scale(key_of[1], (LAYERS, ROWS, COLS), ((0, 4), (1, 2), (2, 4)), -0.2, 0.2), 0.0, 0.5),
        "cap_class": touch_ends(jax.random.randint(key_of[2], (LAYERS, ROWS, COLS), 0, CAP_LEVELS), jax.random.fold_in(key_of[2], 1), 0, CAP_LEVELS - 1).astype(jnp.int32),
        "blocked_mask": touch_ends((jax.random.randint(key_of[3], (LAYERS, ROWS, COLS), 0, 8) < 1).astype(jnp.int32), jax.random.fold_in(key_of[3], 1), 0, 1),
        "fill_start": jnp.clip(1.0 * jax.random.uniform(key_of[4], (LAYERS, ROWS, COLS), jnp.float32) ** block_scale(key_of[4], (LAYERS, ROWS, COLS), ((0, 4), (1, 2), (2, 4)), -0.2, 0.2), 0.0, 1.0),
        "window_dual": gaussian(key_of[5], (LAYERS, ROWS, COLS), 0.5, 4.0, ((0, 4), (1, 2), (2, 4)), jnp.float32),
        "layer_dual": gaussian(key_of[6], (LAYERS, ROWS, COLS), 0.5, 4.0, ((0, 4), (1, 2), (2, 4)), jnp.float32),
    }


step_eta = 0.4
low_density = 0.35
high_density = 0.65
layer_gap = 0.15
tiny_term = 1e-06

def window_sum(field, direction, start):
    extent = field.shape[direction]
    widths = [(0, 0), (0, 0), (0, 0)]
    widths[direction] = (WIN + 1, WIN)
    running = jnp.cumsum(jnp.pad(field, widths), axis=direction)
    upper_sum = lax.slice_in_dim(running, start + 2 * WIN, start + 2 * WIN + extent, axis=direction)
    lower_sum = lax.slice_in_dim(running, start + WIN, start + WIN + extent, axis=direction)
    return upper_sum - lower_sum

def box_sum(field, start):
    return window_sum(window_sum(field, 1, start), 2, start)

def reference(cost_vector, metal_density, cap_class, blocked_mask, fill_start, window_dual, layer_dual):
    layer_count = fill_start.shape[0]
    half_window = WIN // 2
    inverse_area = 1.0 / (WIN * WIN)
    keep_mask = (jnp.arange(layer_count) < layer_count - 1).astype(jnp.float32)[:, None, None]
    capacity = jnp.where(blocked_mask == 1, 0.0, (cap_class + 1).astype(jnp.float32) / CAP_LEVELS)
    has_floor = blocked_mask == 0
    filling = fill_start
    density_dual = window_dual
    stacked_dual = layer_dual * keep_mask
    weight = jnp.float32(1.0)
    for iteration in range(ITERS):
        primal_step = step_eta / weight
        dual_step = step_eta * weight
        earlier = jnp.concatenate([jnp.zeros_like(stacked_dual[:1]), stacked_dual[:-1]], axis=0)
        gradient = cost_vector + box_sum(density_dual, -(WIN - 1 - half_window)) * inverse_area + (stacked_dual - earlier)
        fill_new = jnp.clip(filling - primal_step * gradient, 0.0, capacity)
        moved = fill_new - filling
        level = fill_new + moved + metal_density
        later = jnp.concatenate([level[1:], jnp.zeros_like(level[:1])], axis=0)
        window_term = density_dual / dual_step + box_sum(level, -half_window) * inverse_area
        capped = jnp.minimum(window_term, high_density)
        clipped = jnp.where(has_floor, jnp.maximum(capped, low_density), capped)
        density_new = dual_step * (window_term - clipped)
        layer_term = stacked_dual / dual_step + keep_mask * (level - later)
        stacked_new = dual_step * (layer_term - jnp.clip(layer_term, -layer_gap, layer_gap)) * keep_mask
        primal_sum = jnp.sum(moved * moved)
        dual_sum = jnp.sum((density_new - density_dual) ** 2) + jnp.sum((stacked_new - stacked_dual) ** 2)
        weight = jnp.sqrt(weight) * jnp.sqrt(jnp.sqrt((dual_sum + tiny_term) / (primal_sum + tiny_term)))
        filling = fill_new
        density_dual = density_new
        stacked_dual = stacked_new
    return (filling, density_dual, stacked_dual, weight)
```

```python
import functools

import jax
import jax.numpy as jnp
from jax import lax
from jax.experimental import pallas as pl
from jax.experimental.pallas import tpu as pltpu
from jax.sharding import PartitionSpec as P

WIN = 50
CAP_LEVELS = 8
ITERS = 3

step_eta = 0.4
low_density = 0.35
high_density = 0.65
layer_gap = 0.15
tiny_term = 1e-06

HALF = WIN // 2
HALO = -(-HALF // 16) * 16
TILE = 128
MESH = pl.DeviceIdType.MESH
DIRS = ((-1, 0), (1, 0), (0, -1), (0, 1), (-1, -1), (-1, 1), (1, -1), (1, 1))
ROWS_IN = (0, 1)
REST_IN = (4, 5, 6, 7, 2, 3)
EDGE = (4, 5, 6, 7, 0, 1)
SIDE = (2, 3)
F32 = jnp.float32
BF16 = jnp.bfloat16
NT = (((1,), (1,)), ((), ()))
NN = (((1,), (0,)), ((), ()))


def split(value):
    high = value.astype(BF16)
    low = (value - high.astype(F32)).astype(BF16)
    return high, low


def dot(left, right, dims=NN):
    return lax.dot_general(left, right, dims, preferred_element_type=F32)


def iota(shape, dim):
    return lax.broadcasted_iota(jnp.int32, shape, dim)


def window(offset, start):
    return jnp.where((offset >= start) & (offset < start + WIN), 1.0, 0.0).astype(BF16)


def kernel(
    sizes, cost_in, dens_in, capc_in, blocked_in, x_in, y_in, z_in,
    x, y_out, z, weight_out,
    cost, dens, capc, blocked,
    ext_u, ext_y, et_u, et_y, ht_u, ht_y, above, below, zlow, cap, grad, part,
    band_r, band_h, inner, outer, pick, slots,
    load_sem, send_sem, recv_sem, first_sem, zsend, zrecv, sum_sem, ready,
):
    nl, nr, nc = sizes
    layers, rows, cols = x_in.shape
    top = layers - 1
    ndev = nl * nr * nc
    il, ir, ic = lax.axis_index("layer"), lax.axis_index("row"), lax.axis_index("col")
    me = (il * nr + ir) * nc + ic
    tiles = rows // TILE
    order = list(dict.fromkeys((0, tiles - 1, *range(tiles))))
    ends = order[:2]
    inverse_area = 1.0 / (WIN * WIN)
    own = pl.ds(HALO, rows)
    has_above, has_below = il < nl - 1, il > 0

    pairs = (
        (y_in, ext_y.at[:, own, :]), (z_in, z), (x_in, x), (cost_in, cost), (capc_in, capc),
        (blocked_in, blocked), (dens_in, dens),
    )
    loads = [pltpu.make_async_copy(a, b, load_sem.at[n]) for n, (a, b) in enumerate(pairs)]
    for load in loads:
        load.start()

    for ref in (ext_u, ext_y):
        ref[:, :HALO, :] = jnp.zeros((layers, HALO, cols), F32)
        ref[:, HALO + rows :, :] = jnp.zeros((layers, HALO, cols), F32)
    for ref in (ht_u, ht_y, above, below, zlow):
        ref[...] = jnp.zeros(ref.shape, F32)

    barrier = pltpu.get_barrier_semaphore()

    def ahead(act):
        def one(k, _):
            i = lax.rem(me + k, ndev)
            act((i // (nr * nc), (i // nc) % nr, i % nc))
            return 0

        lax.fori_loop(1, ndev, one, 0, unroll=ndev <= 32)

    def lines(act):
        for n in range(1, nl):
            act((lax.rem(il + n, nl), ir, ic))
        for n in range(1, nr):
            act((il, lax.rem(ir + n, nr), ic))
        for n in range(1, nc):
            act((il, ir, lax.rem(ic + n, nc)))

    line_peers = nl + nr + nc - 3
    corners = []
    for dr, dc in DIRS[4:]:
        there = jnp.logical_and(
            ir < nr - 1 if dr > 0 else ir > 0, ic < nc - 1 if dc > 0 else ic > 0
        )
        corners.append((there, (il, ir + dr, ic + dc)))

    def greet(device):
        pl.semaphore_signal(barrier, inc=1, device_id=device, device_id_type=MESH)

    lines(greet)
    for there, device in corners:
        pl.when(there)(functools.partial(greet, device))

    keep_top = jnp.where(has_above, 1.0, 0.0).astype(F32)
    keep_low = jnp.where(has_below, 1.0, 0.0).astype(F32)
    shape = (2 * HALO, cols)
    k = iota(shape, 0)
    place = jnp.where(k < HALO, k, k - 2 * HALO + cols)
    pick[...] = jnp.where(place == iota(shape, 1), 1.0, 0.0).astype(BF16)

    def span(t, base=0):
        return pl.ds(t * TILE + base, TILE)

    def put_edges(et, l, t, value):
        et[l, :, span(t)] = dot(pick[...], value.astype(BF16), NT)

    loads[0].wait()
    for t in range(tiles):
        for l in range(layers):
            put_edges(et_y, l, t, ext_y[l, span(t, HALO), :])

    pl.semaphore_wait(barrier, line_peers + sum(there.astype(jnp.int32) for there, _ in corners))

    def copies(field):
        ext, et, ht = ((ext_u, et_u, ht_u), (ext_y, et_y, ht_y))[field]
        result = []
        for d, (dr, dc) in enumerate(DIRS):
            from_rows = pl.ds(0 if dc < 0 else HALO, HALO)
            to_rows = pl.ds(HALO if dc < 0 else 0, HALO)

            def ends_of(some, t, dr=dr, dc=dc, from_rows=from_rows, to_rows=to_rows):
                if dc == 0:
                    return (
                        ext.at[some, pl.ds(HALO if dr < 0 else rows, HALO), :],
                        ext.at[some, pl.ds(HALO + rows if dr < 0 else 0, HALO), :],
                    )
                if dr == 0:
                    if t is None:
                        return et.at[some, from_rows, :], ht.at[some, to_rows, pl.ds(TILE, rows)]
                    return et.at[some, from_rows, span(t)], ht.at[some, to_rows, span(t, TILE)]
                if dr < 0:
                    return (
                        et.at[some, from_rows, pl.ds(0, TILE)],
                        ht.at[some, to_rows, pl.ds(TILE + rows, TILE)],
                    )
                return (
                    et.at[some, from_rows, pl.ds(rows - TILE, TILE)],
                    ht.at[some, to_rows, pl.ds(0, TILE)],
                )

            def make(some, t=None, d=d, dr=dr, dc=dc, ends_of=ends_of):
                src, dst = ends_of(some, t)
                return pltpu.make_async_remote_copy(
                    src_ref=src, dst_ref=dst, send_sem=send_sem.at[field, d],
                    recv_sem=recv_sem.at[field, d],
                    device_id=(il, ir + dr, ic + dc), device_id_type=MESH,
                )

            to, frm = [], []
            if dr < 0:
                to.append(ir > 0)
                frm.append(ir < nr - 1)
            if dr > 0:
                to.append(ir < nr - 1)
                frm.append(ir > 0)
            if dc < 0:
                to.append(ic > 0)
                frm.append(ic < nc - 1)
            if dc > 0:
                to.append(ic < nc - 1)
                frm.append(ic > 0)
            result.append(
                (make, functools.reduce(jnp.logical_and, to), functools.reduce(jnp.logical_and, frm))
            )
        return result

    halo_copies = (copies(0), copies(1))
    every = slice(None)

    def begin(field, which, some, t=None):
        for d in which:
            make, to, _ = halo_copies[field][d]
            pl.when(to)(lambda make=make: make(some, t).start())

    def arrived(field, which):
        for d in which:
            make, _, frm = halo_copies[field][d]
            pl.when(frm)(lambda make=make: make(every).wait_recv())

    def departed(field):
        for make, to, _ in halo_copies[field]:
            pl.when(to)(lambda make=make: make(every).wait_send())

    begin(1, SIDE, every)
    begin(1, EDGE, every)

    def first_up(t):
        return pltpu.make_async_remote_copy(
            src_ref=z_in.at[top, span(t), :], dst_ref=zlow.at[span(t), :],
            send_sem=first_sem.at[0, t], recv_sem=first_sem.at[1, t],
            device_id=(il + 1, ir, ic), device_id_type=MESH,
        )

    for t in order:
        pl.when(has_above)(lambda t=t: first_up(t).start())

    def tell(n):
        def one(device):
            pl.semaphore_signal(ready.at[n], inc=1, device_id=device, device_id_type=MESH)

        lines(one)

    tell(0)

    def up(step, t):
        side = step % 2
        return pltpu.make_async_remote_copy(
            src_ref=ext_u.at[top, span(t, HALO), :], dst_ref=below.at[side, span(t), :],
            send_sem=zsend.at[side, 0, t], recv_sem=zrecv.at[side, 0, t],
            device_id=(il + 1, ir, ic), device_id_type=MESH,
        )

    def down(step, t):
        side = step % 2
        return pltpu.make_async_remote_copy(
            src_ref=ext_u.at[0, span(t, HALO), :], dst_ref=above.at[side, span(t), :],
            send_sem=zsend.at[side, 1, t], recv_sem=zrecv.at[side, 1, t],
            device_id=(il - 1, ir, ic), device_id_type=MESH,
        )

    width = layers * 2 * HALO
    for which, start in ((0, -HALF), (1, 1 - HALF)):
        shape = (TILE, TILE + 2 * HALO)
        band_r[which] = window(iota(shape, 1) - HALO - iota(shape, 0), start)
        shape = (TILE, 3 * TILE)
        band_h[which] = window(iota(shape, 1) - TILE - iota(shape, 0), start)
        shape = (cols, cols)
        own_cols = window(iota(shape, 0) - iota(shape, 1), start)
        shape = (2 * HALO, cols)
        k = iota(shape, 0)
        place = jnp.where(k < HALO, k - HALO, k - HALO + cols)
        halo_cols = window(place - iota(shape, 1), start)
        blank = jnp.zeros(shape, BF16)
        for n in range(2):
            inner[which, n * cols : (n + 1) * cols] = own_cols
            for m in range(layers):
                at = n * width + m * 2 * HALO
                for l in range(layers):
                    outer[which, at : at + 2 * HALO, l * cols : (l + 1) * cols] = (
                        halo_cols if m == l else blank
                    )

    def box_own(ext, which, t):
        tall = pl.ds(t * TILE, TILE + 2 * HALO)
        wide = jnp.concatenate([ext[l, tall, :].astype(BF16) for l in range(layers)], axis=1)
        mid = dot(band_r[which], wide)
        pieces = [
            jnp.concatenate(split(mid[:, l * cols : (l + 1) * cols]), axis=1) for l in range(layers)
        ]
        area = dot(jnp.concatenate(pieces, axis=0), inner[which])
        for l in range(layers):
            part[l, span(t), :] = area[l * TILE : (l + 1) * TILE]

    def box_early(field, which):
        ext = (ext_u, ext_y)[field]
        for t in range(tiles):
            if t not in ends:
                box_own(ext, which, t)
        arrived(field, ROWS_IN)
        for t in ends:
            box_own(ext, which, t)
        arrived(field, REST_IN)

    def box_late(ht, which, t):
        halo = ht[:, :, t * TILE : (t + 3) * TILE].reshape(width, 3 * TILE)
        side = dot(band_h[which], halo.astype(BF16), NT)
        area = dot(jnp.concatenate(split(side), axis=1), outer[which])
        return [part[l, span(t), :] + area[:, l * cols : (l + 1) * cols] for l in range(layers)]

    loads[1].wait()
    z[top] = z[top] * keep_top
    for n in range(2, 7):
        loads[n].wait()
    everywhere = [(l, t, (l, span(t), slice(None))) for t in order for l in range(layers)]
    for l, t, at in everywhere:
        level = (capc[at] + 1).astype(F32) * (1.0 / CAP_LEVELS)
        cap[at] = jnp.where(blocked[at] == 1, 0.0, level)

    def fold(value):
        return jnp.sum((value * value).reshape(TILE // 8, 8, cols), axis=0)

    def sums_begin(step, primal_sum, dual_sum):
        slots[step, pl.ds(me, 1)] = jnp.concatenate(
            [jnp.sum(primal_sum, axis=0, keepdims=True), jnp.sum(dual_sum, axis=0, keepdims=True)],
            axis=0,
        )[None]

        def send(device):
            pltpu.make_async_remote_copy(
                src_ref=slots.at[step, me], dst_ref=slots.at[step, me],
                send_sem=sum_sem.at[0, step], recv_sem=sum_sem.at[1, step],
                device_id=device, device_id_type=MESH,
            ).start()

        ahead(send)

    def sums_end(step, weight):
        some = slots.at[step, pl.ds(0, ndev - 1)]
        pltpu.make_async_copy(some, some, sum_sem.at[1, step]).wait()
        pltpu.make_async_copy(some, some, sum_sem.at[0, step]).wait()
        both = jnp.sum(slots[step], axis=0)
        primal = jnp.sum(both[0:1], axis=1, keepdims=True)
        dual = jnp.sum(both[1:2], axis=1, keepdims=True)
        ratio = jnp.broadcast_to((dual + tiny_term) / (primal + tiny_term), (1, cols))
        return jnp.sqrt(weight) * jnp.sqrt(jnp.sqrt(ratio))

    weight = jnp.ones((1, cols), F32)
    for step in range(ITERS):
        last = step == ITERS - 1
        now = step % 2
        count = (tiles * 3 // 4) if step == 0 else tiles // 2
        lower, upper = order[:count], order[count:]

        box_early(1, 1)
        for t in order:
            for l, area in enumerate(box_late(ht_y, 1, t)):
                at = (l, span(t), slice(None))
                value = cost[at] + area * inverse_area + z[at]
                grad[at] = value if l == 0 else value - z[l - 1, span(t), :]
        if step == 0:
            pl.semaphore_wait(ready.at[0], line_peers)
            tell(1)
        if step > 0:
            weight = sums_end(step - 1, weight)
        tau = step_eta / weight
        sigma = step_eta * weight
        sigma_inverse = 1.0 / sigma

        primal_sum = jnp.zeros((8, cols), F32)
        if step == 0:
            sweep = [(l, t) for l in range(1, layers) for t in order] + [(0, t) for t in order]
        else:
            sweep = [(l, t) for t in order for l in reversed(range(layers))]
        for l, t in sweep:
            at = (l, span(t), slice(None))
            slope = grad[at]
            if l == 0:
                if step == 0:
                    pl.when(has_below)(lambda t=t: first_up(t).wait_recv())
                slope = slope - zlow[span(t), :]
            old = x[at]
            new = jnp.minimum(jnp.maximum(old - tau * slope, 0.0), cap[at])
            moved = new - old
            x[at] = new
            primal_sum = primal_sum + fold(moved)
            value = new + moved + dens[at]
            ext_u[l, span(t, HALO), :] = value
            if l == top and t in upper:
                pl.when(has_above)(lambda t=t: up(step, t).start())
            if l == 0:
                pl.when(has_below)(lambda t=t: down(step, t).start())
            put_edges(et_u, l, t, value)
            begin(0, SIDE, l, t)
            if t == ends[-1]:
                begin(0, EDGE, l)
        if not last:
            for t in lower:
                pl.when(has_above)(lambda t=t: up(step, t).start())
        departed(1)
        if step == 0:
            for t in order:
                pl.when(has_above)(lambda t=t: first_up(t).wait_send())

        dual_sum = jnp.zeros((8, cols), F32)

        def update(old, here, later, keep):
            term = old * sigma_inverse + keep * (here - later)
            return sigma * (term - jnp.clip(term, -layer_gap, layer_gap)) * keep

        for l in range(top):
            for t in order:
                at = (l, span(t), slice(None))
                old = z[at]
                new = update(old, ext_u[l, span(t, HALO), :], ext_u[l + 1, span(t, HALO), :], 1.0)
                z[at] = new
                dual_sum = dual_sum + fold(new - old)

        box_early(0, 0)
        for t in order:
            for l, area in enumerate(box_late(ht_u, 0, t)):
                at = (l, span(t), slice(None))
                old = ext_y[l, span(t, HALO), :]
                term = old * sigma_inverse + area * inverse_area
                capped = jnp.minimum(term, high_density)
                clipped = jnp.where(blocked[at] == 0, jnp.maximum(capped, low_density), capped)
                new = sigma * (term - clipped)
                dual_sum = dual_sum + fold(new - old)
                if last:
                    y_out[at] = new
                else:
                    ext_y[l, span(t, HALO), :] = new
                    put_edges(et_y, l, t, new)
                    begin(1, SIDE, l, t)
                    if t == ends[-1]:
                        begin(1, EDGE, l)

        def update_top(t):
            pl.when(has_above)(lambda: down(step, t).wait_recv())
            at = (top, span(t), slice(None))
            old = z[at]
            new = update(old, ext_u[top, span(t, HALO), :], above[now, span(t), :], keep_top)
            z[at] = new
            return fold(new - old)

        def update_low(t):
            pl.when(has_below)(lambda: up(step, t).wait_recv())
            old = zlow[span(t), :]
            new = update(old, below[now, span(t), :], ext_u[0, span(t, HALO), :], keep_low)
            zlow[span(t), :] = new
            return fold(new - old)

        for t in lower:
            dual_sum = dual_sum + update_top(t)
        for t in upper:
            dual_sum = dual_sum + update_low(t)
        if step == 0:
            pl.semaphore_wait(ready.at[1], line_peers)
        sums_begin(step, primal_sum, dual_sum)
        for t in upper:
            update_top(t)
        if not last:
            for t in lower:
                update_low(t)
        for t in order:
            pl.when(has_below)(lambda t=t: down(step, t).wait_send())
            if t in upper or not last:
                pl.when(has_above)(lambda t=t: up(step, t).wait_send())
        departed(0)

    weight_out[...] = sums_end(ITERS - 1, weight)


def flush(*refs):
    count = len(refs) // 2
    ins, outs, sem = refs[:count], refs[count : 2 * count], refs[2 * count]
    moves = [
        pltpu.make_async_copy(a.at[l], b.at[l], sem.at[n, l])
        for n, (a, b) in enumerate(zip(ins, outs))
        for l in range(a.shape[0])
    ]
    for move in moves:
        move.start()
    for move in moves:
        move.wait()


def local(sizes, *args):
    layers, rows, cols = args[0].shape
    ndev = sizes[0] * sizes[1] * sizes[2]
    tiles = rows // TILE
    vmem = pl.BlockSpec(memory_space=pltpu.VMEM)
    anywhere = pl.BlockSpec(memory_space=pl.ANY)
    full = pltpu.VMEM((layers, rows, cols), F32)
    full_int = pltpu.VMEM((layers, rows, cols), jnp.int32)
    line = pltpu.VMEM((1, cols), F32)
    ext = pltpu.VMEM((layers, rows + 2 * HALO, cols), F32)
    et = pltpu.VMEM((layers, 2 * HALO, rows), F32)
    ht = pltpu.VMEM((layers, 2 * HALO, rows + 2 * TILE), F32)
    plane = pltpu.VMEM((rows, cols), F32)
    planes = pltpu.VMEM((2, rows, cols), F32)
    x, y, z, weight = pl.pallas_call(
        functools.partial(kernel, sizes),
        out_shape=(full, full, full, line),
        in_specs=[anywhere] * 7,
        out_specs=(vmem,) * 4,
        scratch_shapes=[
            full, full, full_int, full_int,
            ext, ext, et, et, ht, ht, planes, planes, plane, full, full, full,
            pltpu.VMEM((2, TILE, TILE + 2 * HALO), BF16),
            pltpu.VMEM((2, TILE, 3 * TILE), BF16),
            pltpu.VMEM((2, 2 * cols, cols), BF16),
            pltpu.VMEM((2, 2 * layers * 2 * HALO, layers * cols), BF16),
            pltpu.VMEM((2 * HALO, cols), BF16),
            pltpu.VMEM((ITERS, ndev, 2, cols), F32),
            pltpu.SemaphoreType.DMA((7,)),
            pltpu.SemaphoreType.DMA((2, 8)),
            pltpu.SemaphoreType.DMA((2, 8)),
            pltpu.SemaphoreType.DMA((2, tiles)),
            pltpu.SemaphoreType.DMA((2, 2, tiles)),
            pltpu.SemaphoreType.DMA((2, 2, tiles)),
            pltpu.SemaphoreType.DMA((2, ITERS)),
            pltpu.SemaphoreType.REGULAR((2,)),
        ],
        compiler_params=pltpu.CompilerParams(collective_id=0, has_side_effects=True),
        name="fill_steps",
    )(*args)
    whole = jax.ShapeDtypeStruct((layers, rows, cols), F32)
    x, y, z = pl.pallas_call(
        flush,
        out_shape=(whole,) * 3,
        in_specs=[anywhere] * 3,
        out_specs=(anywhere,) * 3,
        scratch_shapes=[pltpu.SemaphoreType.DMA((3, layers))],
        name="flush",
    )(*(pltpu.with_memory_space_constraint(value, pltpu.VMEM) for value in (x, y, z)))
    return x, y, z, weight[0, 0]


def solution(mesh):
    sizes = tuple(mesh.shape[axis] for axis in ("layer", "row", "col"))
    spec = P("layer", "row", "col")
    return jax.shard_map(
        functools.partial(local, sizes),
        mesh=mesh,
        in_specs=(spec,) * 7,
        out_specs=(spec, spec, spec, P()),
        check_vma=False,
    )
```

```python
import functools

import jax
import jax.numpy as jnp
from jax import lax
from jax.experimental import pallas as pl
from jax.experimental.pallas import tpu as pltpu
from jax.sharding import PartitionSpec as P

WIN = 50
CAP_LEVELS = 8
ITERS = 3

step_eta = 0.4
low_density = 0.35
high_density = 0.65
layer_gap = 0.15
tiny_term = 1e-06

HALF = WIN // 2
HALO = -(-HALF // 16) * 16
TILE = 128
MESH = pl.DeviceIdType.MESH
HBM = "hbm"
DIRS = ((-1, 0), (1, 0), (0, -1), (0, 1), (-1, -1), (-1, 1), (1, -1), (1, 1))
ROWS = (0, 1)
SIDE = (2, 3)
CORNER = (4, 5, 6, 7)
F32 = jnp.float32
BF16 = jnp.bfloat16
NT = (((1,), (1,)), ((), ()))
NN = (((1,), (0,)), ((), ()))


def split(value):
    high = value.astype(BF16)
    low = (value - high.astype(F32)).astype(BF16)
    return high, low


def dot(left, right, dims=NN):
    return lax.dot_general(left, right, dims, preferred_element_type=F32)


def iota(shape, dim):
    return lax.broadcasted_iota(jnp.int32, shape, dim)


def window(offset, start):
    return jnp.where((offset >= start) & (offset < start + WIN), 1.0, 0.0).astype(BF16)


def spreads(sizes):
    distance, result = 1, []
    while distance < max(sizes) - 1:
        result.append(distance)
        distance *= 2
    return result


def kernel(
    sizes, cost_in, dens_in, capc_in, blocked_in, x_in, y_in, z_in,
    x, y_out, z, weight_out,
    reals, flags,
    ext_u, ext_y, et_u, et_y, ht_u, ht_y, ct_u, ct_y, above, below, zlow, cap, grad, part,
    band_r, band_h, inner, outer, pick, slots,
    load_sem, send_sem, recv_sem, first_sem, zsend, zrecv, sum_sem, ready,
):
    nl, nr, nc = sizes
    layers, rows, cols = x_in.shape
    top = layers - 1
    ndev = nl * nr * nc
    il, ir, ic = lax.axis_index("layer"), lax.axis_index("row"), lax.axis_index("col")
    me = (il * nr + ir) * nc + ic
    cost, dens, capc, blocked = reals.at[0], reals.at[1], flags.at[0], flags.at[1]
    tiles = rows // TILE
    order = list(dict.fromkeys((0, tiles - 1, *range(tiles))))
    ends = order[:2]
    rest = order[2:]
    inverse_area = 1.0 / (WIN * WIN)
    own = pl.ds(HALO, rows)
    has_above, has_below = il < nl - 1, il > 0

    pairs = (
        (y_in, ext_y.at[:, own, :], 0), (z_in, z, 1), (cost_in, cost, 2), (dens_in, dens, 2),
        (x_in, x, 3), (capc_in, capc, 4), (blocked_in, blocked, 4),
    )
    for a, b, n in pairs:
        pltpu.make_async_copy(a, b, load_sem.at[n]).start()
    loads = [
        pltpu.make_async_copy(ref, ref, load_sem.at[n])
        for n, ref in enumerate((ext_y.at[:, own, :], z, reals, x, flags))
    ]

    for ref in (ext_u, ext_y):
        ref[:, :HALO, :] = jnp.zeros((layers, HALO, cols), F32)
        ref[:, HALO + rows :, :] = jnp.zeros((layers, HALO, cols), F32)
    for ref in (ht_u, ht_y, ct_u, ct_y, above, below, zlow):
        ref[...] = jnp.zeros(ref.shape, F32)

    barrier = pltpu.get_barrier_semaphore()

    def ahead(act):
        def one(k, _):
            i = lax.rem(me + k, ndev)
            act((i // (nr * nc), (i // nc) % nr, i % nc))
            return 0

        lax.fori_loop(1, ndev, one, 0, unroll=ndev <= 32)

    def lines(act):
        for n in range(1, nl):
            act((lax.rem(il + n, nl), ir, ic))
        for n in range(1, nr):
            act((il, lax.rem(ir + n, nr), ic))
        for n in range(1, nc):
            act((il, ir, lax.rem(ic + n, nc)))

    def beside(distance):
        peers = []
        for axis, (at, n) in enumerate(((il, nl), (ir, nr), (ic, nc))):
            if distance < n:
                for there, to in ((at >= distance, at - distance), (at < n - distance, at + distance)):
                    device = [il, ir, ic]
                    device[axis] = to
                    peers.append((there, tuple(device)))
        return peers

    line_peers = nl + nr + nc - 3
    corners = []
    for dr, dc in DIRS[4:]:
        there = jnp.logical_and(
            ir < nr - 1 if dr > 0 else ir > 0, ic < nc - 1 if dc > 0 else ic > 0
        )
        corners.append((there, (il, ir + dr, ic + dc)))

    def signal(semaphore, device):
        pl.semaphore_signal(semaphore, inc=1, device_id=device, device_id_type=MESH)

    def signal_some(semaphore, peers):
        for there, device in peers:
            pl.when(there)(functools.partial(signal, semaphore, device))

    def wait_some(semaphore, peers):
        pl.semaphore_wait(semaphore, sum(there.astype(jnp.int32) for there, _ in peers))

    signal_some(barrier, beside(1) + corners)

    spread = spreads(sizes)
    rounds = len(spread) + 2

    def tell(n):
        if n < len(spread):
            signal_some(ready.at[n], beside(spread[n]))
        elif n < rounds:
            lines(functools.partial(signal, ready.at[n]))

    def hear(n):
        if n < len(spread):
            wait_some(ready.at[n], beside(spread[n]))
        elif n < rounds:
            pl.semaphore_wait(ready.at[n], line_peers)
        tell(n + 1)

    def span(t, base=0):
        return pl.ds(t * TILE + base, TILE)

    wait_some(barrier, beside(1) + corners)

    def first_up(t):
        return pltpu.make_async_remote_copy(
            src_ref=z_in.at[top, span(t), :], dst_ref=zlow.at[span(t), :],
            send_sem=first_sem.at[tiles], recv_sem=first_sem.at[t],
            device_id=(il + 1, ir, ic), device_id_type=MESH,
        )

    @pl.when(has_above)
    def _():
        for t in order:
            first_up(t).start()


    tell(0)

    keep_top = jnp.where(has_above, 1.0, 0.0).astype(F32)
    keep_low = jnp.where(has_below, 1.0, 0.0).astype(F32)
    shape = (2 * HALO, cols)
    k = iota(shape, 0)
    place = jnp.where(k < HALO, k, k - 2 * HALO + cols)
    pick[...] = jnp.where(place == iota(shape, 1), 1.0, 0.0).astype(BF16)

    def put_edges(et, l, t, value):
        turned = value.T
        et[l, :HALO, span(t)] = turned[:HALO]
        et[l, HALO:, span(t)] = turned[cols - HALO :]

    def put_corners(ct, first, final):
        blank = jnp.zeros((TILE - layers * HALO, cols), F32)
        for n, pieces in enumerate(
            ([value[:HALO] for value in first], [value[TILE - HALO :] for value in final])
        ):
            ct[0, n] = dot(pick[...], jnp.concatenate(pieces + [blank], axis=0).astype(BF16), NT)

    def take_corners(ct, ht):
        for l in range(layers):
            ht[l, :, :TILE] = pltpu.roll(ct[1, 1], TILE - (l + 1) * HALO, axis=1)
            last_tile = ct[1, 0]
            ht[l, :, TILE + rows :] = pltpu.roll(last_tile, TILE - l * HALO, axis=1) if l else last_tile

    def copies(field):
        ext, et, ht, ct = ((ext_u, et_u, ht_u, ct_u), (ext_y, et_y, ht_y, ct_y))[field]
        result = []
        for d, (dr, dc) in enumerate(DIRS):
            from_rows = pl.ds(0 if dc < 0 else HALO, HALO)
            to_rows = pl.ds(HALO if dc < 0 else 0, HALO)

            def ends_of(some, t, dr=dr, dc=dc, from_rows=from_rows, to_rows=to_rows):
                if dc == 0:
                    return (
                        y_in.at[some, pl.ds(0 if dr < 0 else rows - HALO, HALO), :] if t is HBM
                        else ext.at[some, pl.ds(HALO if dr < 0 else rows, HALO), :],
                        ext.at[some, pl.ds(HALO + rows if dr < 0 else 0, HALO), :],
                    )
                if dr == 0:
                    if t is None:
                        return et.at[some, from_rows, :], ht.at[some, to_rows, pl.ds(TILE, rows)]
                    return et.at[some, from_rows, span(t)], ht.at[some, to_rows, span(t, TILE)]
                n = 0 if dr < 0 else 1
                return ct.at[0, n, from_rows, :], ct.at[1, n, to_rows, :]

            def make(some, t=None, d=d, dr=dr, dc=dc, ends_of=ends_of):
                src, dst = ends_of(some, t)
                return pltpu.make_async_remote_copy(
                    src_ref=src, dst_ref=dst, send_sem=send_sem.at[field, d],
                    recv_sem=recv_sem.at[field, d],
                    device_id=(il, ir + dr, ic + dc), device_id_type=MESH,
                )

            to, frm = [], []
            if dr < 0:
                to.append(ir > 0)
                frm.append(ir < nr - 1)
            if dr > 0:
                to.append(ir < nr - 1)
                frm.append(ir > 0)
            if dc < 0:
                to.append(ic > 0)
                frm.append(ic < nc - 1)
            if dc > 0:
                to.append(ic < nc - 1)
                frm.append(ic > 0)
            result.append(
                (make, functools.reduce(jnp.logical_and, to), functools.reduce(jnp.logical_and, frm))
            )
        return result

    halo_copies = (copies(0), copies(1))
    every = slice(None)

    def begin(field, which, some, some_tiles=(None,)):
        for d in which:
            make, to, _ = halo_copies[field][d]

            @pl.when(to)
            def _(make=make):
                for t in some_tiles:
                    make(some, t).start()

    def arrived(field, which):
        for d in which:
            make, _, frm = halo_copies[field][d]
            pl.when(frm)(lambda make=make: make(every).wait_recv())

    def departed(field):
        for make, to, _ in halo_copies[field]:
            pl.when(to)(lambda make=make: make(every).wait_send())

    begin(1, ROWS, every, (HBM,))
    loads[0].wait()
    for t in range(tiles):
        for l in range(layers):
            put_edges(et_y, l, t, ext_y[l, span(t, HALO), :])
    put_corners(
        ct_y,
        [ext_y[l, span(0, HALO), :] for l in range(layers)],
        [ext_y[l, span(tiles - 1, HALO), :] for l in range(layers)],
    )
    begin(1, SIDE + CORNER, every)

    def lower_of(step):
        return order[: tiles // 2]

    def up(step, t):
        side = step % 2
        return pltpu.make_async_remote_copy(
            src_ref=ext_u.at[top, span(t, HALO), :], dst_ref=below.at[side, span(t), :],
            send_sem=zsend.at[side, 0], recv_sem=zrecv.at[side, 0, int(t in lower_of(step))],
            device_id=(il + 1, ir, ic), device_id_type=MESH,
        )

    def down(step, t):
        side = step % 2
        return pltpu.make_async_remote_copy(
            src_ref=ext_u.at[0, span(t, HALO), :], dst_ref=above.at[side, span(t), :],
            send_sem=zsend.at[side, 1], recv_sem=zrecv.at[side, 1, int(t not in lower_of(step))],
            device_id=(il - 1, ir, ic), device_id_type=MESH,
        )

    width = layers * 2 * HALO
    for which, start in ((0, -HALF), (1, 1 - HALF)):
        shape = (TILE, TILE + 2 * HALO)
        band_r[which] = window(iota(shape, 1) - HALO - iota(shape, 0), start)
        shape = (TILE, 3 * TILE)
        band_h[which] = window(iota(shape, 1) - TILE - iota(shape, 0), start)
        shape = (cols, cols)
        own_cols = window(iota(shape, 0) - iota(shape, 1), start)
        shape = (2 * HALO, cols)
        k = iota(shape, 0)
        place = jnp.where(k < HALO, k - HALO, k - HALO + cols)
        halo_cols = window(place - iota(shape, 1), start)
        blank = jnp.zeros(shape, BF16)
        for n in range(2):
            inner[which, n * cols : (n + 1) * cols] = own_cols
            for m in range(layers):
                at = n * width + m * 2 * HALO
                for l in range(layers):
                    outer[which, at : at + 2 * HALO, l * cols : (l + 1) * cols] = (
                        halo_cols if m == l else blank
                    )

    def box_own(ext, which, t):
        tall = pl.ds(t * TILE, TILE + 2 * HALO)
        wide = jnp.concatenate([ext[l, tall, :].astype(BF16) for l in range(layers)], axis=1)
        mid = dot(band_r[which], wide)
        pieces = [
            jnp.concatenate(split(mid[:, l * cols : (l + 1) * cols]), axis=1) for l in range(layers)
        ]
        area = dot(jnp.concatenate(pieces, axis=0), inner[which])
        for l in range(layers):
            part[l, span(t), :] = area[l * TILE : (l + 1) * TILE]

    def box_early(field, which, then=None):
        ext = (ext_u, ext_y)[field]
        for t in range(tiles):
            if t not in ends:
                box_own(ext, which, t)
        arrived(field, ROWS)
        if then is not None:
            then()
        for t in ends:
            box_own(ext, which, t)
        arrived(field, CORNER + SIDE)
        take_corners((ct_u, ct_y)[field], (ht_u, ht_y)[field])

    def box_late(ht, which, t):
        halo = ht[:, :, t * TILE : (t + 3) * TILE].reshape(width, 3 * TILE)
        side = dot(band_h[which], halo.astype(BF16), NT)
        area = dot(jnp.concatenate(split(side), axis=1), outer[which])
        return [part[l, span(t), :] + area[:, l * cols : (l + 1) * cols] for l in range(layers)]

    loads[1].wait()
    z[top] = z[top] * keep_top
    for load in loads[2:]:
        load.wait()
    everywhere = [(l, t, (l, span(t), slice(None))) for t in order for l in range(layers)]
    for l, t, at in everywhere:
        level = (capc[at] + 1).astype(F32) * (1.0 / CAP_LEVELS)
        cap[at] = jnp.where(blocked[at] == 1, 0.0, level)

    def fold(value):
        return jnp.sum((value * value).reshape(TILE // 8, 8, cols), axis=0)

    def sums_begin(step, primal_sum, dual_sum):
        slots[step, pl.ds(me, 1)] = jnp.concatenate(
            [jnp.sum(primal_sum, axis=0, keepdims=True), jnp.sum(dual_sum, axis=0, keepdims=True)],
            axis=0,
        )[None]

        def send(device):
            pltpu.make_async_remote_copy(
                src_ref=slots.at[step, me], dst_ref=slots.at[step, me],
                send_sem=sum_sem.at[0, step], recv_sem=sum_sem.at[1, step],
                device_id=device, device_id_type=MESH,
            ).start()

        ahead(send)

    def sums_end(step, weight):
        some = slots.at[step, pl.ds(0, ndev - 1)]
        pltpu.make_async_copy(some, some, sum_sem.at[1, step]).wait()
        pltpu.make_async_copy(some, some, sum_sem.at[0, step]).wait()
        both = jnp.sum(slots[step], axis=0)
        primal = jnp.sum(both[0:1], axis=1, keepdims=True)
        dual = jnp.sum(both[1:2], axis=1, keepdims=True)
        ratio = jnp.broadcast_to((dual + tiny_term) / (primal + tiny_term), (1, cols))
        return jnp.sqrt(weight) * jnp.sqrt(jnp.sqrt(ratio))

    weight = jnp.ones((1, cols), F32)
    for step in range(ITERS):
        last = step == ITERS - 1
        now = step % 2
        lower = lower_of(step)
        upper = [t for t in order if t not in lower]

        box_early(1, 1)
        for t in order:
            for l, area in enumerate(box_late(ht_y, 1, t)):
                at = (l, span(t), slice(None))
                grad[at] = cost[at] + area * inverse_area
        if step > 0:
            finish()
            weight = sums_end(step - 1, weight)
        tau = step_eta / weight
        sigma = step_eta * weight
        sigma_inverse = 1.0 / sigma

        primal_sum = jnp.zeros((8, cols), F32)
        groups = [g for g in (ends, rest) if g]
        if step == 0:
            blocks = [(range(1, layers), g) for g in groups] + [(range(1), [t]) for t in order]
        else:
            blocks = [(range(layers), g) for g in groups]
        if step == 0:
            hear(0)
        for some_layers, some_tiles in blocks:
            if step == 0 and 0 in some_layers:
                for t in some_tiles:
                    pl.when(has_below)(lambda t=t: first_up(t).wait_recv())
            for t in some_tiles:
                for l in some_layers:
                    at = (l, span(t), slice(None))
                    earlier = zlow[span(t), :] if l == 0 else z[l - 1, span(t), :]
                    slope = grad[at] + (z[at] - earlier)
                    old = x[at]
                    new = jnp.minimum(jnp.maximum(old - tau * slope, 0.0), cap[at])
                    moved = new - old
                    x[at] = new
                    primal_sum = primal_sum + fold(moved)
                    value = new + moved + dens[at]
                    ext_u[l, span(t, HALO), :] = value
                    put_edges(et_u, l, t, value)
            first_layer = some_layers[0]
            some = pl.ds(first_layer, len(some_layers))
            corner_ready = 0 in some_layers and ends[-1] in some_tiles
            if corner_ready:
                put_corners(
                    ct_u,
                    [ext_u[l, span(0, HALO), :] for l in range(layers)],
                    [ext_u[l, span(tiles - 1, HALO), :] for l in range(layers)],
                )
            begin(0, SIDE, some, some_tiles)
            if ends[-1] in some_tiles:
                begin(0, ROWS, some)
            if corner_ready:
                begin(0, CORNER, every)
            if 0 in some_layers:

                @pl.when(has_below)
                def _(step=step, some_tiles=some_tiles):
                    for t in some_tiles:
                        if t in lower:
                            down(step, t).start()

            if top in some_layers:
                going = [t for t in some_tiles if t in upper]

                @pl.when(has_above)
                def _(step=step, going=going):
                    for t in going:
                        up(step, t).start()

            if step == 0:
                if (some_layers, some_tiles) == blocks[1]:
                    hear(1)
        departed(1)
        if step == 0:

            pl.when(has_above)(pltpu.make_async_copy(zlow, zlow, first_sem.at[tiles]).wait)

        dual_sum = jnp.zeros((8, cols), F32)

        def update(old, here, later, keep, sigma=sigma, sigma_inverse=sigma_inverse):
            term = old * sigma_inverse + keep * (here - later)
            return sigma * (term - jnp.clip(term, -layer_gap, layer_gap)) * keep

        for l in range(top):
            for t in order:
                at = (l, span(t), slice(None))
                old = z[at]
                new = update(old, ext_u[l, span(t, HALO), :], ext_u[l + 1, span(t, HALO), :], 1.0)
                z[at] = new
                dual_sum = dual_sum + fold(new - old)

        def other_half(last=last, step=step, lower=lower, upper=upper):
            @pl.when(has_below)
            def _():
                for t in upper:
                    down(step, t).start()

            if not last:

                @pl.when(has_above)
                def _():
                    for t in lower:
                        up(step, t).start()

        box_early(0, 0, other_half)
        if step == 0:
            hear(2)
        for t in order:
            if not last and rest and t == rest[0]:
                put_corners(
                    ct_y,
                    [ext_y[l, span(0, HALO), :] for l in range(layers)],
                    [ext_y[l, span(tiles - 1, HALO), :] for l in range(layers)],
                )
                begin(1, SIDE, every, ends)
                begin(1, ROWS + CORNER, every)
            for l, area in enumerate(box_late(ht_u, 0, t)):
                at = (l, span(t), slice(None))
                old = ext_y[l, span(t, HALO), :]
                term = old * sigma_inverse + area * inverse_area
                capped = jnp.minimum(term, high_density)
                clipped = jnp.where(blocked[at] == 0, jnp.maximum(capped, low_density), capped)
                new = sigma * (term - clipped)
                dual_sum = dual_sum + fold(new - old)
                if last:
                    y_out[at] = new
                else:
                    ext_y[l, span(t, HALO), :] = new
                    put_edges(et_y, l, t, new)

        if not last:
            begin(1, SIDE, every, rest)

        def update_top(t, now=now, update=update):
            at = (top, span(t), slice(None))
            old = z[at]
            new = update(old, ext_u[top, span(t, HALO), :], above[now, span(t), :], keep_top)
            z[at] = new
            return fold(new - old)

        def update_low(t, now=now, update=update):
            old = zlow[span(t), :]
            new = update(old, below[now, span(t), :], ext_u[0, span(t, HALO), :], keep_low)
            zlow[span(t), :] = new
            return fold(new - old)

        def landed(downs, ups, now=now, lower=lower):
            for there, plane, way, some in (
                (has_above, above, 1, downs), (has_below, below, 0, ups)
            ):
                if some:
                    all_of = plane.at[now, pl.ds(0, len(some) * TILE), :]
                    which = int((some == lower) == (way == 0))
                    pl.when(there)(
                        pltpu.make_async_copy(all_of, all_of, zrecv.at[now, way, which]).wait
                    )

        landed(lower, upper)
        for t in lower:
            dual_sum = dual_sum + update_top(t)
        for t in upper:
            dual_sum = dual_sum + update_low(t)
        if step == 0:
            for n in range(3, rounds):
                hear(n)
        sums_begin(step, primal_sum, dual_sum)

        def finish(last=last, step=step, now=now, lower=lower, upper=upper, landed=landed,
                   update_top=update_top, update_low=update_low):
            landed(upper, [] if last else lower)
            for t in upper:
                update_top(t)
            if not last:
                for t in lower:
                    update_low(t)

            for there, way, gone in ((has_below, 1, order), (has_above, 0, upper if last else order)):
                all_of = above.at[now, pl.ds(0, len(gone) * TILE), :]
                pl.when(there)(pltpu.make_async_copy(all_of, all_of, zsend.at[now, way]).wait)

            departed(0)

    finish()
    weight_out[...] = sums_end(ITERS - 1, weight)


def flush(*refs):
    count = len(refs) // 2
    ins, outs, sem = refs[:count], refs[count : 2 * count], refs[2 * count]
    moves = [
        pltpu.make_async_copy(a.at[l], b.at[l], sem.at[n, l])
        for n, (a, b) in enumerate(zip(ins, outs))
        for l in range(a.shape[0])
    ]
    for move in moves:
        move.start()
    for move in moves:
        move.wait()


def local(sizes, *args):
    layers, rows, cols = args[0].shape
    ndev = sizes[0] * sizes[1] * sizes[2]
    tiles = rows // TILE
    vmem = pl.BlockSpec(memory_space=pltpu.VMEM)
    anywhere = pl.BlockSpec(memory_space=pl.ANY)
    full = pltpu.VMEM((layers, rows, cols), F32)
    fields = pltpu.VMEM((2, layers, rows, cols), F32)
    field_flags = pltpu.VMEM((2, layers, rows, cols), jnp.int32)
    line = pltpu.VMEM((1, cols), F32)
    ext = pltpu.VMEM((layers, rows + 2 * HALO, cols), F32)
    et = pltpu.VMEM((layers, 2 * HALO, rows), F32)
    ht = pltpu.VMEM((layers, 2 * HALO, rows + 2 * TILE), F32)
    ct = pltpu.VMEM((2, 2, 2 * HALO, TILE), F32)
    plane = pltpu.VMEM((rows, cols), F32)
    planes = pltpu.VMEM((2, rows, cols), F32)
    x, y, z, weight = pl.pallas_call(
        functools.partial(kernel, sizes),
        out_shape=(full, full, full, line),
        in_specs=[anywhere] * 7,
        out_specs=(vmem,) * 4,
        scratch_shapes=[
            fields, field_flags,
            ext, ext, et, et, ht, ht, ct, ct, planes, planes, plane, full, full, full,
            pltpu.VMEM((2, TILE, TILE + 2 * HALO), BF16),
            pltpu.VMEM((2, TILE, 3 * TILE), BF16),
            pltpu.VMEM((2, 2 * cols, cols), BF16),
            pltpu.VMEM((2, 2 * layers * 2 * HALO, layers * cols), BF16),
            pltpu.VMEM((2 * HALO, cols), BF16),
            pltpu.VMEM((ITERS, ndev, 2, cols), F32),
            pltpu.SemaphoreType.DMA((5,)),
            pltpu.SemaphoreType.DMA((2, 8)),
            pltpu.SemaphoreType.DMA((2, 8)),
            pltpu.SemaphoreType.DMA((tiles + 1,)),
            pltpu.SemaphoreType.DMA((2, 2)),
            pltpu.SemaphoreType.DMA((2, 2, 2)),
            pltpu.SemaphoreType.DMA((2, ITERS)),
            pltpu.SemaphoreType.REGULAR((len(spreads(sizes)) + 2,)),
        ],
        compiler_params=pltpu.CompilerParams(collective_id=0, has_side_effects=True),
        name="fill_steps",
    )(*args)
    whole = jax.ShapeDtypeStruct((layers, rows, cols), F32)
    x, y, z = pl.pallas_call(
        flush,
        out_shape=(whole,) * 3,
        in_specs=[anywhere] * 3,
        out_specs=(anywhere,) * 3,
        scratch_shapes=[pltpu.SemaphoreType.DMA((3, layers))],
        name="flush",
    )(*(pltpu.with_memory_space_constraint(value, pltpu.VMEM) for value in (x, y, z)))
    return x, y, z, weight[0, 0]


def solution(mesh):
    sizes = tuple(mesh.shape[axis] for axis in ("layer", "row", "col"))
    spec = P("layer", "row", "col")
    return jax.shard_map(
        functools.partial(local, sizes),
        mesh=mesh,
        in_specs=(spec,) * 7,
        out_specs=(spec, spec, spec, P()),
        check_vma=False,
    )
```

```python
import functools

import jax
import jax.numpy as jnp
from jax import lax
from jax.experimental import pallas as pl
from jax.experimental.pallas import tpu as pltpu
from jax.sharding import PartitionSpec as P

WIN = 50
CAP_LEVELS = 8
ITERS = 3

step_eta = 0.4
low_density = 0.35
high_density = 0.65
layer_gap = 0.15
tiny_term = 1e-06

HALF = WIN // 2
HALO = -(-HALF // 16) * 16
MOST = (HALF - 1) // 8 * 8
assert WIN == 2 * HALF and MOST == HALF - 1
TILE = 128
MESH = pl.DeviceIdType.MESH
HBM, EXTRA = "hbm", "extra"
DIRS = ((-1, 0), (1, 0), (0, -1), (0, 1), (-1, -1), (-1, 1), (1, -1), (1, 1))
ROWS = (0, 1)
SIDE = (2, 3)
CORNER = (4, 5, 6, 7)
F32 = jnp.float32
BF16 = jnp.bfloat16
NT = (((1,), (1,)), ((), ()))
NN = (((1,), (0,)), ((), ()))


def split(value):
    high = value.astype(BF16)
    low = (value - high.astype(F32)).astype(BF16)
    return high, low


def dot(left, right, dims=NN):
    return lax.dot_general(left, right, dims, preferred_element_type=F32)


def iota(shape, dim):
    return lax.broadcasted_iota(jnp.int32, shape, dim)


def window(offset, start):
    return jnp.where((offset >= start) & (offset < start + WIN), 1.0, 0.0).astype(BF16)


def spreads(sizes):
    distance, result = 1, []
    while distance < max(sizes) - 1:
        result.append(distance)
        distance *= 2
    return result


def kernel(
    sizes, cost_in, dens_in, capc_in, blocked_in, x_in, y_in, z_in,
    x, y_out, z, weight_out,
    reals, flags,
    ext_u, ext_y, et_u, et_y, ht_u, ht_y, ct_u, ct_y, ex_u, ex_y, above, below, zlow, cap, grad, part,
    band_r, band_h, inner, outer, pick, slots,
    load_sem, send_sem, recv_sem, first_sem, zsend, zrecv, sum_sem, ready,
):
    nl, nr, nc = sizes
    layers, rows, cols = x_in.shape
    top = layers - 1
    ndev = nl * nr * nc
    il, ir, ic = lax.axis_index("layer"), lax.axis_index("row"), lax.axis_index("col")
    me = (il * nr + ir) * nc + ic
    cost, dens, capc, blocked = reals.at[0], reals.at[1], flags.at[0], flags.at[1]
    tiles = rows // TILE
    order = list(dict.fromkeys((0, tiles - 1, *range(tiles))))
    ends = order[:2]
    rest = order[2:]
    inverse_area = 1.0 / (WIN * WIN)
    own = pl.ds(HALO, rows)
    has_above, has_below = il < nl - 1, il > 0

    pairs = (
        (y_in, ext_y.at[:, own, :], 0), (z_in, z, 1), (cost_in, cost, 2), (dens_in, dens, 2),
        (x_in, x, 3), (capc_in, capc, 4), (blocked_in, blocked, 4),
    )
    for a, b, n in pairs:
        pltpu.make_async_copy(a, b, load_sem.at[n]).start()
    loads = [
        pltpu.make_async_copy(ref, ref, load_sem.at[n])
        for n, ref in enumerate((ext_y.at[:, own, :], z, reals, x, flags))
    ]

    for ref in (ext_u, ext_y):
        ref[:, :HALO, :] = jnp.zeros((layers, HALO, cols), F32)
        ref[:, HALO + rows :, :] = jnp.zeros((layers, HALO, cols), F32)
    for ref in (ht_u, ht_y, ct_u, ct_y, ex_u, ex_y, above, below, zlow):
        ref[...] = jnp.zeros(ref.shape, F32)

    barrier = pltpu.get_barrier_semaphore()

    def ahead(act):
        def one(k, _):
            i = lax.rem(me + k, ndev)
            act((i // (nr * nc), (i // nc) % nr, i % nc))
            return 0

        lax.fori_loop(1, ndev, one, 0, unroll=ndev <= 32)

    def lines(act):
        for n in range(1, nl):
            act((lax.rem(il + n, nl), ir, ic))
        for n in range(1, nr):
            act((il, lax.rem(ir + n, nr), ic))
        for n in range(1, nc):
            act((il, ir, lax.rem(ic + n, nc)))

    def beside(distance):
        peers = []
        for axis, (at, n) in enumerate(((il, nl), (ir, nr), (ic, nc))):
            if distance < n:
                for there, to in ((at >= distance, at - distance), (at < n - distance, at + distance)):
                    device = [il, ir, ic]
                    device[axis] = to
                    peers.append((there, tuple(device)))
        return peers

    line_peers = nl + nr + nc - 3
    corners = []
    for dr, dc in DIRS[4:]:
        there = jnp.logical_and(
            ir < nr - 1 if dr > 0 else ir > 0, ic < nc - 1 if dc > 0 else ic > 0
        )
        corners.append((there, (il, ir + dr, ic + dc)))

    def signal(semaphore, device):
        pl.semaphore_signal(semaphore, inc=1, device_id=device, device_id_type=MESH)

    def signal_some(semaphore, peers):
        for there, device in peers:
            pl.when(there)(functools.partial(signal, semaphore, device))

    def wait_some(semaphore, peers):
        pl.semaphore_wait(semaphore, sum(there.astype(jnp.int32) for there, _ in peers))

    signal_some(barrier, beside(1) + corners)

    spread = spreads(sizes)
    rounds = len(spread) + 2

    def tell(n):
        if n < len(spread):
            signal_some(ready.at[n], beside(spread[n]))
        elif n < rounds:
            lines(functools.partial(signal, ready.at[n]))

    def hear(n):
        if n < len(spread):
            wait_some(ready.at[n], beside(spread[n]))
        elif n < rounds:
            pl.semaphore_wait(ready.at[n], line_peers)
        tell(n + 1)

    def span(t, base=0):
        return pl.ds(t * TILE + base, TILE)

    wait_some(barrier, beside(1) + corners)

    def first_up(t):
        return pltpu.make_async_remote_copy(
            src_ref=z_in.at[top, span(t), :], dst_ref=zlow.at[span(t), :],
            send_sem=first_sem.at[tiles], recv_sem=first_sem.at[t],
            device_id=(il + 1, ir, ic), device_id_type=MESH,
        )

    @pl.when(has_above)
    def _():
        for t in order:
            first_up(t).start()


    tell(0)

    keep_top = jnp.where(has_above, 1.0, 0.0).astype(F32)
    keep_low = jnp.where(has_below, 1.0, 0.0).astype(F32)
    shape = (2 * HALO, cols)
    k = iota(shape, 0)
    place = jnp.where(k < HALO, k, k - 2 * HALO + cols)
    pick[...] = jnp.where(place == iota(shape, 1), 1.0, 0.0).astype(BF16)

    def put_edges(field, l, t, value):
        et, ex = ((et_u, ex_u), (et_y, ex_y))[field]
        turned = value.T
        beyond = cols - HALF if field == 0 else HALF - 1
        ex[0, l : l + 1, span(t)] = turned[beyond : beyond + 1]
        et[l, :HALO, span(t)] = turned[:HALO]
        et[l, HALO:, span(t)] = turned[cols - HALO :]

    def put_corners(ct, first, final):
        blank = jnp.zeros((TILE - layers * HALO, cols), F32)
        for n, pieces in enumerate(
            ([value[:HALO] for value in first], [value[TILE - HALO :] for value in final])
        ):
            ct[0, n] = dot(pick[...], jnp.concatenate(pieces + [blank], axis=0).astype(BF16), NT)

    def take_corners(ct, ht):
        for l in range(layers):
            ht[l, :, :TILE] = pltpu.roll(ct[1, 1], TILE - (l + 1) * HALO, axis=1)
            last_tile = ct[1, 0]
            ht[l, :, TILE + rows :] = pltpu.roll(last_tile, TILE - l * HALO, axis=1) if l else last_tile

    def copies(field):
        ext, et, ht, ct, ex = (
            (ext_u, et_u, ht_u, ct_u, ex_u), (ext_y, et_y, ht_y, ct_y, ex_y)
        )[field]
        longer = 1 if field == 0 else -1
        result = []
        for d, (dr, dc) in enumerate(DIRS):
            wide = HALO if dr and dc == longer else MOST
            from_rows = pl.ds(0 if dc < 0 else 2 * HALO - wide, wide)
            to_rows = pl.ds(HALO if dc < 0 else HALO - wide, wide)
            tall = HALO if dr == longer else MOST

            def ends_of(some, t, dr=dr, dc=dc, from_rows=from_rows, to_rows=to_rows, tall=tall):
                if dc == 0:
                    return (
                        y_in.at[some, pl.ds(0 if dr < 0 else rows - tall, tall), :] if t is HBM
                        else ext.at[some, pl.ds(HALO if dr < 0 else HALO + rows - tall, tall), :],
                        ext.at[some, pl.ds(HALO + rows if dr < 0 else HALO - tall, tall), :],
                    )
                if dr == 0:
                    if t is EXTRA:
                        return ex.at[0], ex.at[1]
                    if t is None:
                        return et.at[some, from_rows, :], ht.at[some, to_rows, pl.ds(TILE, rows)]
                    return et.at[some, from_rows, span(t)], ht.at[some, to_rows, span(t, TILE)]
                n = 0 if dr < 0 else 1
                return ct.at[0, n, from_rows, :], ct.at[1, n, to_rows, :]

            def make(some, t=None, d=d, dr=dr, dc=dc, ends_of=ends_of):
                src, dst = ends_of(some, t)
                return pltpu.make_async_remote_copy(
                    src_ref=src, dst_ref=dst, send_sem=send_sem.at[field, d],
                    recv_sem=recv_sem.at[field, d],
                    device_id=(il, ir + dr, ic + dc), device_id_type=MESH,
                )

            to, frm = [], []
            if dr < 0:
                to.append(ir > 0)
                frm.append(ir < nr - 1)
            if dr > 0:
                to.append(ir < nr - 1)
                frm.append(ir > 0)
            if dc < 0:
                to.append(ic > 0)
                frm.append(ic < nc - 1)
            if dc > 0:
                to.append(ic < nc - 1)
                frm.append(ic > 0)

            def both(semaphore, d=d):
                size = above.at[0, pl.ds(0, layers * HALF * rows // cols), :]
                return pltpu.make_async_copy(size, size, semaphore.at[field, d])

            if dr or dc != longer:
                both = None

            result.append(
                (make, both, functools.reduce(jnp.logical_and, to), functools.reduce(jnp.logical_and, frm))
            )
        return result

    halo_copies = (copies(0), copies(1))
    every = slice(None)

    def begin(field, which, some, some_tiles=(None,), whole=False):
        for d in which:
            make, both, to, _ = halo_copies[field][d]

            @pl.when(to)
            def _(make=make, both=both):
                for t in some_tiles:
                    make(some, t).start()
                if whole and both:
                    make(every, EXTRA).start()

    def arrived(field, which):
        for d in which:
            make, both, _, frm = halo_copies[field][d]
            pl.when(frm)(
                lambda make=make, both=both: (both(recv_sem).wait() if both else make(every).wait_recv())
            )

    def departed(field):
        for make, both, to, _ in halo_copies[field]:
            pl.when(to)(
                lambda make=make, both=both: (both(send_sem).wait() if both else make(every).wait_send())
            )

    begin(1, ROWS, every, (HBM,))
    loads[0].wait()
    for t in range(tiles):
        for l in range(layers):
            put_edges(1, l, t, ext_y[l, span(t, HALO), :])
    put_corners(
        ct_y,
        [ext_y[l, span(0, HALO), :] for l in range(layers)],
        [ext_y[l, span(tiles - 1, HALO), :] for l in range(layers)],
    )
    begin(1, SIDE + CORNER, every, whole=True)

    def lower_of(step):
        return order[::2]

    def up(step, t):
        side = step % 2
        return pltpu.make_async_remote_copy(
            src_ref=ext_u.at[top, span(t, HALO), :], dst_ref=below.at[side, span(t), :],
            send_sem=zsend.at[side, 0], recv_sem=zrecv.at[side, 0, int(t in lower_of(step))],
            device_id=(il + 1, ir, ic), device_id_type=MESH,
        )

    def down(step, t):
        side = step % 2
        return pltpu.make_async_remote_copy(
            src_ref=ext_u.at[0, span(t, HALO), :], dst_ref=above.at[side, span(t), :],
            send_sem=zsend.at[side, 1], recv_sem=zrecv.at[side, 1, int(t not in lower_of(step))],
            device_id=(il - 1, ir, ic), device_id_type=MESH,
        )

    width = layers * 2 * HALO
    for which, start in ((0, -HALF), (1, 1 - HALF)):
        shape = (TILE, TILE + 2 * HALO)
        band_r[which] = window(iota(shape, 1) - HALO - iota(shape, 0), start)
        shape = (TILE, 3 * TILE)
        band_h[which] = window(iota(shape, 1) - TILE - iota(shape, 0), start)
        shape = (cols, cols)
        own_cols = window(iota(shape, 0) - iota(shape, 1), start)
        shape = (2 * HALO, cols)
        k = iota(shape, 0)
        place = jnp.where(k < HALO, k - HALO, k - HALO + cols)
        halo_cols = window(place - iota(shape, 1), start)
        blank = jnp.zeros(shape, BF16)
        for n in range(2):
            inner[which, n * cols : (n + 1) * cols] = own_cols
            for m in range(layers):
                at = n * width + m * 2 * HALO
                for l in range(layers):
                    outer[which, at : at + 2 * HALO, l * cols : (l + 1) * cols] = (
                        halo_cols if m == l else blank
                    )

    def box_own(ext, which, t):
        tall = pl.ds(t * TILE, TILE + 2 * HALO)
        wide = jnp.concatenate([ext[l, tall, :].astype(BF16) for l in range(layers)], axis=1)
        mid = dot(band_r[which], wide)
        pieces = [
            jnp.concatenate(split(mid[:, l * cols : (l + 1) * cols]), axis=1) for l in range(layers)
        ]
        area = dot(jnp.concatenate(pieces, axis=0), inner[which])
        for l in range(layers):
            part[l, span(t), :] = area[l * TILE : (l + 1) * TILE]

    def box_early(field, which):
        ext = (ext_u, ext_y)[field]
        for t in range(tiles):
            if t not in ends:
                box_own(ext, which, t)
        arrived(field, ROWS)
        for t in ends:
            box_own(ext, which, t)
        arrived(field, CORNER + SIDE)
        ht, ex = ((ht_u, ex_u), (ht_y, ex_y))[field]
        take_corners((ct_u, ct_y)[field], ht)
        row = HALO - HALF if field == 0 else HALO + HALF - 1
        for l in range(layers):
            ht[l, row : row + 1, TILE : TILE + rows] = ex[1, l : l + 1]

    def box_late(ht, which, t):
        halo = ht[:, :, t * TILE : (t + 3) * TILE].reshape(width, 3 * TILE)
        side = dot(band_h[which], halo.astype(BF16), NT)
        area = dot(jnp.concatenate(split(side), axis=1), outer[which])
        return [part[l, span(t), :] + area[:, l * cols : (l + 1) * cols] for l in range(layers)]

    loads[1].wait()
    z[top] = z[top] * keep_top
    for load in loads[2:]:
        load.wait()
    everywhere = [(l, t, (l, span(t), slice(None))) for t in order for l in range(layers)]
    for l, t, at in everywhere:
        level = (capc[at] + 1).astype(F32) * (1.0 / CAP_LEVELS)
        cap[at] = jnp.where(blocked[at] == 1, 0.0, level)

    def fold(value):
        return jnp.sum((value * value).reshape(TILE // 8, 8, cols), axis=0)

    def sums_begin(step, primal_sum, dual_sum):
        slots[step, pl.ds(me, 1)] = jnp.concatenate(
            [jnp.sum(primal_sum, axis=0, keepdims=True), jnp.sum(dual_sum, axis=0, keepdims=True)],
            axis=0,
        )[None]

        def send(device):
            pltpu.make_async_remote_copy(
                src_ref=slots.at[step, me], dst_ref=slots.at[step, me],
                send_sem=sum_sem.at[0, step], recv_sem=sum_sem.at[1, step],
                device_id=device, device_id_type=MESH,
            ).start()

        ahead(send)

    def sums_end(step, weight):
        some = slots.at[step, pl.ds(0, ndev - 1)]
        pltpu.make_async_copy(some, some, sum_sem.at[1, step]).wait()
        pltpu.make_async_copy(some, some, sum_sem.at[0, step]).wait()
        both = jnp.sum(slots[step], axis=0)
        primal = jnp.sum(both[0:1], axis=1, keepdims=True)
        dual = jnp.sum(both[1:2], axis=1, keepdims=True)
        ratio = jnp.broadcast_to((dual + tiny_term) / (primal + tiny_term), (1, cols))
        return jnp.sqrt(weight) * jnp.sqrt(jnp.sqrt(ratio))

    weight = jnp.ones((1, cols), F32)
    for step in range(ITERS):
        last = step == ITERS - 1
        now = step % 2
        lower = lower_of(step)
        upper = [t for t in order if t not in lower]

        box_early(1, 1)
        for t in order:
            for l, area in enumerate(box_late(ht_y, 1, t)):
                at = (l, span(t), slice(None))
                grad[at] = cost[at] + area * inverse_area
        if step > 0:
            finish()
            weight = sums_end(step - 1, weight)
        tau = step_eta / weight
        sigma = step_eta * weight
        sigma_inverse = 1.0 / sigma

        primal_sum = jnp.zeros((8, cols), F32)
        groups = [g for g in (ends, rest) if g]
        if step == 0:
            blocks = [(range(1, layers), g) for g in groups] + [(range(1), [t]) for t in order]
        else:
            blocks = [(range(layers), g) for g in groups]
        if step == 0:
            hear(0)
        for some_layers, some_tiles in blocks:
            if step == 0 and 0 in some_layers:
                for t in some_tiles:
                    pl.when(has_below)(lambda t=t: first_up(t).wait_recv())
            for t in some_tiles:
                for l in some_layers:
                    at = (l, span(t), slice(None))
                    earlier = zlow[span(t), :] if l == 0 else z[l - 1, span(t), :]
                    slope = grad[at] + (z[at] - earlier)
                    old = x[at]
                    new = jnp.minimum(jnp.maximum(old - tau * slope, 0.0), cap[at])
                    moved = new - old
                    x[at] = new
                    primal_sum = primal_sum + fold(moved)
                    value = new + moved + dens[at]
                    ext_u[l, span(t, HALO), :] = value
                    put_edges(0, l, t, value)
            first_layer = some_layers[0]
            some = pl.ds(first_layer, len(some_layers))
            corner_ready = 0 in some_layers and ends[-1] in some_tiles
            if corner_ready:
                put_corners(
                    ct_u,
                    [ext_u[l, span(0, HALO), :] for l in range(layers)],
                    [ext_u[l, span(tiles - 1, HALO), :] for l in range(layers)],
                )
            if 0 in some_layers:

                @pl.when(has_below)
                def _(step=step, some_tiles=some_tiles):
                    for t in some_tiles:
                        if t in lower:
                            down(step, t).start()

            if top in some_layers:
                going = [t for t in some_tiles if t in upper]

                @pl.when(has_above)
                def _(step=step, going=going):
                    for t in going:
                        up(step, t).start()

            begin(0, SIDE, some, some_tiles, (some_layers, some_tiles) == blocks[-1])
            if ends[-1] in some_tiles:
                begin(0, ROWS, some)
            if corner_ready:
                begin(0, CORNER, every)
            if step == 0:
                if (some_layers, some_tiles) == blocks[1]:
                    hear(1)
        departed(1)
        if step == 0:

            pl.when(has_above)(pltpu.make_async_copy(zlow, zlow, first_sem.at[tiles]).wait)

        dual_sum = jnp.zeros((8, cols), F32)

        def update(old, here, later, keep, sigma=sigma, sigma_inverse=sigma_inverse):
            term = old * sigma_inverse + keep * (here - later)
            return sigma * (term - jnp.clip(term, -layer_gap, layer_gap)) * keep

        for l in range(top):
            for t in order:
                at = (l, span(t), slice(None))
                old = z[at]
                new = update(old, ext_u[l, span(t, HALO), :], ext_u[l + 1, span(t, HALO), :], 1.0)
                z[at] = new
                dual_sum = dual_sum + fold(new - old)

        def other_half(n, last=last, step=step, lower=lower, upper=upper):
            @pl.when(has_below)
            def _():
                for t in upper[n::2]:
                    down(step, t).start()

            if not last:

                @pl.when(has_above)
                def _():
                    for t in lower[n::2]:
                        up(step, t).start()

        box_early(0, 0)
        other_half(0)
        if step == 0:
            hear(2)
        for t in order:
            if not last and rest and t == rest[0]:
                put_corners(
                    ct_y,
                    [ext_y[l, span(0, HALO), :] for l in range(layers)],
                    [ext_y[l, span(tiles - 1, HALO), :] for l in range(layers)],
                )
                begin(1, SIDE, every, ends)
                begin(1, ROWS + CORNER, every)
            for l, area in enumerate(box_late(ht_u, 0, t)):
                at = (l, span(t), slice(None))
                old = ext_y[l, span(t, HALO), :]
                term = old * sigma_inverse + area * inverse_area
                capped = jnp.minimum(term, high_density)
                clipped = jnp.where(blocked[at] == 0, jnp.maximum(capped, low_density), capped)
                new = sigma * (term - clipped)
                dual_sum = dual_sum + fold(new - old)
                if last:
                    y_out[at] = new
                else:
                    ext_y[l, span(t, HALO), :] = new
                    put_edges(1, l, t, new)

        if not last:
            begin(1, SIDE, every, rest, True)

        def update_top(t, now=now, update=update):
            at = (top, span(t), slice(None))
            old = z[at]
            new = update(old, ext_u[top, span(t, HALO), :], above[now, span(t), :], keep_top)
            z[at] = new
            return fold(new - old)

        def update_low(t, now=now, update=update):
            old = zlow[span(t), :]
            new = update(old, below[now, span(t), :], ext_u[0, span(t, HALO), :], keep_low)
            zlow[span(t), :] = new
            return fold(new - old)

        def landed(downs, ups, now=now, lower=lower):
            for there, plane, way, some in (
                (has_above, above, 1, downs), (has_below, below, 0, ups)
            ):
                if some:
                    all_of = plane.at[now, pl.ds(0, len(some) * TILE), :]
                    which = int((some == lower) == (way == 0))
                    pl.when(there)(
                        pltpu.make_async_copy(all_of, all_of, zrecv.at[now, way, which]).wait
                    )

        landed(lower, upper)
        for t in lower:
            dual_sum = dual_sum + update_top(t)
        for t in upper:
            dual_sum = dual_sum + update_low(t)
        if step == 0:
            for n in range(3, rounds):
                hear(n)
        sums_begin(step, primal_sum, dual_sum)
        other_half(1)

        def finish(last=last, step=step, now=now, lower=lower, upper=upper, landed=landed,
                   update_top=update_top, update_low=update_low):
            landed(upper, [] if last else lower)
            for t in upper:
                update_top(t)
            if not last:
                for t in lower:
                    update_low(t)

            for there, way, gone in ((has_below, 1, order), (has_above, 0, upper if last else order)):
                all_of = above.at[now, pl.ds(0, len(gone) * TILE), :]
                pl.when(there)(pltpu.make_async_copy(all_of, all_of, zsend.at[now, way]).wait)

            departed(0)

    finish()
    weight_out[...] = sums_end(ITERS - 1, weight)


def flush(*refs):
    count = len(refs) // 2
    ins, outs, sem = refs[:count], refs[count : 2 * count], refs[2 * count]
    moves = [
        pltpu.make_async_copy(a.at[l], b.at[l], sem.at[n, l])
        for n, (a, b) in enumerate(zip(ins, outs))
        for l in range(a.shape[0])
    ]
    for move in moves:
        move.start()
    for move in moves:
        move.wait()


def local(sizes, *args):
    layers, rows, cols = args[0].shape
    ndev = sizes[0] * sizes[1] * sizes[2]
    tiles = rows // TILE
    vmem = pl.BlockSpec(memory_space=pltpu.VMEM)
    anywhere = pl.BlockSpec(memory_space=pl.ANY)
    full = pltpu.VMEM((layers, rows, cols), F32)
    fields = pltpu.VMEM((2, layers, rows, cols), F32)
    field_flags = pltpu.VMEM((2, layers, rows, cols), jnp.int32)
    line = pltpu.VMEM((1, cols), F32)
    ext = pltpu.VMEM((layers, rows + 2 * HALO, cols), F32)
    et = pltpu.VMEM((layers, 2 * HALO, rows), F32)
    ht = pltpu.VMEM((layers, 2 * HALO, rows + 2 * TILE), F32)
    ct = pltpu.VMEM((2, 2, 2 * HALO, TILE), F32)
    ex = pltpu.VMEM((2, layers, rows), F32)
    plane = pltpu.VMEM((rows, cols), F32)
    planes = pltpu.VMEM((2, rows, cols), F32)
    x, y, z, weight = pl.pallas_call(
        functools.partial(kernel, sizes),
        out_shape=(full, full, full, line),
        in_specs=[anywhere] * 7,
        out_specs=(vmem,) * 4,
        scratch_shapes=[
            fields, field_flags,
            ext, ext, et, et, ht, ht, ct, ct, ex, ex, planes, planes, plane, full, full, full,
            pltpu.VMEM((2, TILE, TILE + 2 * HALO), BF16),
            pltpu.VMEM((2, TILE, 3 * TILE), BF16),
            pltpu.VMEM((2, 2 * cols, cols), BF16),
            pltpu.VMEM((2, 2 * layers * 2 * HALO, layers * cols), BF16),
            pltpu.VMEM((2 * HALO, cols), BF16),
            pltpu.VMEM((ITERS, ndev, 2, cols), F32),
            pltpu.SemaphoreType.DMA((5,)),
            pltpu.SemaphoreType.DMA((2, 8)),
            pltpu.SemaphoreType.DMA((2, 8)),
            pltpu.SemaphoreType.DMA((tiles + 1,)),
            pltpu.SemaphoreType.DMA((2, 2)),
            pltpu.SemaphoreType.DMA((2, 2, 2)),
            pltpu.SemaphoreType.DMA((2, ITERS)),
            pltpu.SemaphoreType.REGULAR((len(spreads(sizes)) + 2,)),
        ],
        compiler_params=pltpu.CompilerParams(collective_id=0, has_side_effects=True),
        name="fill_steps",
    )(*args)
    whole = jax.ShapeDtypeStruct((layers, rows, cols), F32)
    x, y, z = pl.pallas_call(
        flush,
        out_shape=(whole,) * 3,
        in_specs=[anywhere] * 3,
        out_specs=(anywhere,) * 3,
        scratch_shapes=[pltpu.SemaphoreType.DMA((3, layers))],
        name="flush",
    )(*(pltpu.with_memory_space_constraint(value, pltpu.VMEM) for value in (x, y, z)))
    return x, y, z, weight[0, 0]


def solution(mesh):
    sizes = tuple(mesh.shape[axis] for axis in ("layer", "row", "col"))
    spec = P("layer", "row", "col")
    return jax.shard_map(
        functools.partial(local, sizes),
        mesh=mesh,
        in_specs=(spec,) * 7,
        out_specs=(spec, spec, spec, P()),
        check_vma=False,
    )
```

```python
import functools

import jax
import jax.numpy as jnp
from jax import lax
from jax.experimental import pallas as pl
from jax.experimental.pallas import tpu as pltpu
from jax.sharding import PartitionSpec as P

WIN = 50
CAP_LEVELS = 8
ITERS = 3

step_eta = 0.4
low_density = 0.35
high_density = 0.65
layer_gap = 0.15
tiny_term = 1e-06

HALF = WIN // 2
HALO = -(-HALF // 16) * 16
MOST = (HALF - 1) // 8 * 8
assert WIN == 2 * HALF and MOST == HALF - 1
TILE = 128
MESH = pl.DeviceIdType.MESH
HBM, EXTRA = "hbm", "extra"
DIRS = ((-1, 0), (1, 0), (0, -1), (0, 1), (-1, -1), (-1, 1), (1, -1), (1, 1))
ROWS = (0, 1)
SIDE = (2, 3)
CORNER = (4, 5, 6, 7)
F32 = jnp.float32
BF16 = jnp.bfloat16
NT = (((1,), (1,)), ((), ()))
NN = (((1,), (0,)), ((), ()))


def split(value):
    high = value.astype(BF16)
    low = (value - high.astype(F32)).astype(BF16)
    return high, low


def dot(left, right, dims=NN):
    return lax.dot_general(left, right, dims, preferred_element_type=F32)


def iota(shape, dim):
    return lax.broadcasted_iota(jnp.int32, shape, dim)


def window(offset, start):
    return jnp.where((offset >= start) & (offset < start + WIN), 1.0, 0.0).astype(BF16)


def spreads(sizes):
    distance, result = 1, []
    while distance < max(sizes) - 1:
        result.append(distance)
        distance *= 2
    return result


def kernel(
    sizes, cost_in, dens_in, capc_in, blocked_in, x_in, y_in, z_in,
    x, y_out, z, weight_out,
    reals, flags,
    ext_u, ext_y, et_u, et_y, ht_u, ht_y, ct_u, ct_y, ex_u, ex_y, above, below, zlow, cap, grad, part,
    band_r, band_h, inner, outer, pick, slots,
    load_sem, send_sem, recv_sem, first_sem, zsend, zrecv, sum_sem, ready,
):
    nl, nr, nc = sizes
    layers, rows, cols = x_in.shape
    top = layers - 1
    ndev = nl * nr * nc
    il, ir, ic = lax.axis_index("layer"), lax.axis_index("row"), lax.axis_index("col")
    me = (il * nr + ir) * nc + ic
    cost, dens, capc, blocked = reals.at[0], reals.at[1], flags.at[0], flags.at[1]
    tiles = rows // TILE
    order = list(dict.fromkeys((0, tiles - 1, *range(tiles))))
    ends = order[:2]
    rest = order[2:]
    inverse_area = 1.0 / (WIN * WIN)
    own = pl.ds(HALO, rows)
    has_above, has_below = il < nl - 1, il > 0

    pairs = (
        (y_in, ext_y.at[:, own, :], 0), (z_in, z, 1), (cost_in, cost, 2), (dens_in, dens, 2),
        (x_in, x, 3), (capc_in, capc, 4), (blocked_in, blocked, 4),
    )
    loads = [
        pltpu.make_async_copy(ref, ref, load_sem.at[n])
        for n, ref in enumerate((ext_y.at[:, own, :], z, reals, x, flags))
    ]

    for ref in (ext_u, ext_y):
        ref[:, :HALO, :] = jnp.zeros((layers, HALO, cols), F32)
        ref[:, HALO + rows :, :] = jnp.zeros((layers, HALO, cols), F32)
    for ref in (ht_u, ht_y, ct_u, ct_y, ex_u, ex_y):
        ref[...] = jnp.zeros(ref.shape, F32)

    barrier = pltpu.get_barrier_semaphore()

    def ahead(act):
        def one(k, _):
            i = lax.rem(me + k, ndev)
            act((i // (nr * nc), (i // nc) % nr, i % nc))
            return 0

        lax.fori_loop(1, ndev, one, 0, unroll=ndev <= 32)

    def lines(act):
        for n in range(1, nl):
            act((lax.rem(il + n, nl), ir, ic))
        for n in range(1, nr):
            act((il, lax.rem(ir + n, nr), ic))
        for n in range(1, nc):
            act((il, ir, lax.rem(ic + n, nc)))

    def beside(distance):
        peers = []
        for axis, (at, n) in enumerate(((il, nl), (ir, nr), (ic, nc))):
            if distance < n:
                for there, to in ((at >= distance, at - distance), (at < n - distance, at + distance)):
                    device = [il, ir, ic]
                    device[axis] = to
                    peers.append((there, tuple(device)))
        return peers

    line_peers = nl + nr + nc - 3
    corners = []
    for dr, dc in DIRS[4:]:
        there = jnp.logical_and(
            ir < nr - 1 if dr > 0 else ir > 0, ic < nc - 1 if dc > 0 else ic > 0
        )
        corners.append((there, (il, ir + dr, ic + dc)))

    def signal(semaphore, device):
        pl.semaphore_signal(semaphore, inc=1, device_id=device, device_id_type=MESH)

    def signal_some(semaphore, peers):
        for there, device in peers:
            pl.when(there)(functools.partial(signal, semaphore, device))

    def wait_some(semaphore, peers):
        pl.semaphore_wait(semaphore, sum(there.astype(jnp.int32) for there, _ in peers))

    signal_some(barrier, beside(1) + corners)
    for a, b, n in pairs:
        pltpu.make_async_copy(a, b, load_sem.at[n]).start()

    @pl.when(jnp.logical_not(has_above))
    def _():
        above[...] = jnp.zeros(above.shape, F32)

    @pl.when(jnp.logical_not(has_below))
    def _():
        below[...] = jnp.zeros(below.shape, F32)
        zlow[...] = jnp.zeros(zlow.shape, F32)

    spread = spreads(sizes)
    rounds = len(spread) + 2

    def tell(n):
        if n < len(spread):
            signal_some(ready.at[n], beside(spread[n]))
        elif n < rounds:
            lines(functools.partial(signal, ready.at[n]))

    def hear(n):
        if n < len(spread):
            wait_some(ready.at[n], beside(spread[n]))
        elif n < rounds:
            pl.semaphore_wait(ready.at[n], line_peers)
        tell(n + 1)

    def span(t, base=0):
        return pl.ds(t * TILE + base, TILE)

    wait_some(barrier, beside(1) + corners)

    def first_up(t):
        return pltpu.make_async_remote_copy(
            src_ref=z.at[top, span(t), :], dst_ref=zlow.at[span(t), :],
            send_sem=first_sem.at[tiles], recv_sem=first_sem.at[t],
            device_id=(il + 1, ir, ic), device_id_type=MESH,
        )

    loads[1].wait()

    @pl.when(has_above)
    def _():
        for t in order:
            first_up(t).start()


    tell(0)

    keep_top = jnp.where(has_above, 1.0, 0.0).astype(F32)
    keep_low = jnp.where(has_below, 1.0, 0.0).astype(F32)
    shape = (2 * HALO, cols)
    k = iota(shape, 0)
    place = jnp.where(k < HALO, k, k - 2 * HALO + cols)
    pick[...] = jnp.where(place == iota(shape, 1), 1.0, 0.0).astype(BF16)

    def put_edges(field, l, t, value):
        et, ex = ((et_u, ex_u), (et_y, ex_y))[field]
        turned = value.T
        beyond = cols - HALF if field == 0 else HALF - 1
        ex[0, l : l + 1, span(t)] = turned[beyond : beyond + 1]
        et[l, :HALO, span(t)] = turned[:HALO]
        et[l, HALO:, span(t)] = turned[cols - HALO :]

    def put_corners(ct, first, final):
        blank = jnp.zeros((TILE - layers * HALO, cols), F32)
        for n, pieces in enumerate(
            ([value[:HALO] for value in first], [value[TILE - HALO :] for value in final])
        ):
            ct[0, n] = dot(pick[...], jnp.concatenate(pieces + [blank], axis=0).astype(BF16), NT)

    def take_corners(ct, ht):
        for l in range(layers):
            ht[l, :, :TILE] = pltpu.roll(ct[1, 1], TILE - (l + 1) * HALO, axis=1)
            last_tile = ct[1, 0]
            ht[l, :, TILE + rows :] = pltpu.roll(last_tile, TILE - l * HALO, axis=1) if l else last_tile

    def copies(field):
        ext, et, ht, ct, ex = (
            (ext_u, et_u, ht_u, ct_u, ex_u), (ext_y, et_y, ht_y, ct_y, ex_y)
        )[field]
        longer = 1 if field == 0 else -1
        result = []
        for d, (dr, dc) in enumerate(DIRS):
            wide = HALO if dr and dc == longer else MOST
            from_rows = pl.ds(0 if dc < 0 else 2 * HALO - wide, wide)
            to_rows = pl.ds(HALO if dc < 0 else HALO - wide, wide)
            tall = HALO if dr == longer else MOST

            def ends_of(some, t, dr=dr, dc=dc, from_rows=from_rows, to_rows=to_rows, tall=tall):
                if dc == 0:
                    return (
                        y_in.at[some, pl.ds(0 if dr < 0 else rows - tall, tall), :] if t is HBM
                        else ext.at[some, pl.ds(HALO if dr < 0 else HALO + rows - tall, tall), :],
                        ext.at[some, pl.ds(HALO + rows if dr < 0 else HALO - tall, tall), :],
                    )
                if dr == 0:
                    if t is EXTRA:
                        return ex.at[0], ex.at[1]
                    if t is None:
                        return et.at[some, from_rows, :], ht.at[some, to_rows, pl.ds(TILE, rows)]
                    return et.at[some, from_rows, span(t)], ht.at[some, to_rows, span(t, TILE)]
                n = 0 if dr < 0 else 1
                return ct.at[0, n, from_rows, :], ct.at[1, n, to_rows, :]

            def make(some, t=None, d=d, dr=dr, dc=dc, ends_of=ends_of):
                src, dst = ends_of(some, t)
                return pltpu.make_async_remote_copy(
                    src_ref=src, dst_ref=dst, send_sem=send_sem.at[field, d],
                    recv_sem=recv_sem.at[field, d],
                    device_id=(il, ir + dr, ic + dc), device_id_type=MESH,
                )

            to, frm = [], []
            if dr < 0:
                to.append(ir > 0)
                frm.append(ir < nr - 1)
            if dr > 0:
                to.append(ir < nr - 1)
                frm.append(ir > 0)
            if dc < 0:
                to.append(ic > 0)
                frm.append(ic < nc - 1)
            if dc > 0:
                to.append(ic < nc - 1)
                frm.append(ic > 0)

            def both(semaphore, d=d):
                size = above.at[0, pl.ds(0, layers * HALF * rows // cols), :]
                return pltpu.make_async_copy(size, size, semaphore.at[field, d])

            if dr or dc != longer:
                both = None

            result.append(
                (make, both, functools.reduce(jnp.logical_and, to), functools.reduce(jnp.logical_and, frm))
            )
        return result

    halo_copies = (copies(0), copies(1))
    every = slice(None)

    def begin(field, which, some, some_tiles=(None,), whole=False):
        for d in which:
            make, both, to, _ = halo_copies[field][d]

            @pl.when(to)
            def _(make=make, both=both):
                for t in some_tiles:
                    make(some, t).start()
                if whole and both:
                    make(every, EXTRA).start()

    def arrived(field, which):
        for d in which:
            make, both, _, frm = halo_copies[field][d]
            pl.when(frm)(
                lambda make=make, both=both: (both(recv_sem).wait() if both else make(every).wait_recv())
            )

    def departed(field):
        for make, both, to, _ in halo_copies[field]:
            pl.when(to)(
                lambda make=make, both=both: (both(send_sem).wait() if both else make(every).wait_send())
            )

    begin(1, ROWS, every, (HBM,))
    loads[0].wait()
    for t in range(tiles):
        for l in range(layers):
            put_edges(1, l, t, ext_y[l, span(t, HALO), :])
    put_corners(
        ct_y,
        [ext_y[l, span(0, HALO), :] for l in range(layers)],
        [ext_y[l, span(tiles - 1, HALO), :] for l in range(layers)],
    )
    begin(1, SIDE + CORNER, every, whole=True)

    lower, upper = order[::2], order[1::2]

    def portion(t, way):
        if t in (upper, lower)[way]:
            return 0
        return 1 + (lower, upper)[way].index(t) % 2

    def up(step, t):
        side = step % 2
        return pltpu.make_async_remote_copy(
            src_ref=ext_u.at[top, span(t, HALO), :], dst_ref=below.at[side, span(t), :],
            send_sem=zsend.at[side, 0], recv_sem=zrecv.at[side, 0, portion(t, 0)],
            device_id=(il + 1, ir, ic), device_id_type=MESH,
        )

    def down(step, t):
        side = step % 2
        return pltpu.make_async_remote_copy(
            src_ref=ext_u.at[0, span(t, HALO), :], dst_ref=above.at[side, span(t), :],
            send_sem=zsend.at[side, 1], recv_sem=zrecv.at[side, 1, portion(t, 1)],
            device_id=(il - 1, ir, ic), device_id_type=MESH,
        )

    width = layers * 2 * HALO
    for which, start in ((0, -HALF), (1, 1 - HALF)):
        shape = (TILE, TILE + 2 * HALO)
        band_r[which] = window(iota(shape, 1) - HALO - iota(shape, 0), start)
        shape = (TILE, 3 * TILE)
        band_h[which] = window(iota(shape, 1) - TILE - iota(shape, 0), start)
        shape = (cols, cols)
        own_cols = window(iota(shape, 0) - iota(shape, 1), start)
        shape = (2 * HALO, cols)
        k = iota(shape, 0)
        place = jnp.where(k < HALO, k - HALO, k - HALO + cols)
        halo_cols = window(place - iota(shape, 1), start)
        blank = jnp.zeros(shape, BF16)
        for n in range(2):
            inner[which, n * cols : (n + 1) * cols] = own_cols
            for m in range(layers):
                at = n * width + m * 2 * HALO
                for l in range(layers):
                    outer[which, at : at + 2 * HALO, l * cols : (l + 1) * cols] = (
                        halo_cols if m == l else blank
                    )

    def box_own(ext, which, some_tiles):
        pieces = []
        for t in some_tiles:
            tall = pl.ds(t * TILE, TILE + 2 * HALO)
            wide = jnp.concatenate([ext[l, tall, :].astype(BF16) for l in range(layers)], axis=1)
            mid = dot(band_r[which], wide)
            pieces += [
                jnp.concatenate(split(mid[:, l * cols : (l + 1) * cols]), axis=1)
                for l in range(layers)
            ]
        area = dot(jnp.concatenate(pieces, axis=0), inner[which])
        for n, t in enumerate(some_tiles):
            for l in range(layers):
                at = (n * layers + l) * TILE
                part[l, span(t), :] = area[at : at + TILE]

    def box_early(field, which):
        ext = (ext_u, ext_y)[field]
        if rest:
            box_own(ext, which, rest)
        arrived(field, ROWS)
        box_own(ext, which, ends)
        arrived(field, CORNER + SIDE)
        ht, ex = ((ht_u, ex_u), (ht_y, ex_y))[field]
        take_corners((ct_u, ct_y)[field], ht)
        row = HALO - HALF if field == 0 else HALO + HALF - 1
        for l in range(layers):
            ht[l, row : row + 1, TILE : TILE + rows] = ex[1, l : l + 1]

    def box_late(ht, which, some_tiles):
        halo = jnp.concatenate(
            [ht[:, :, t * TILE : (t + 3) * TILE].reshape(width, 3 * TILE) for t in some_tiles], axis=0
        )
        side = dot(band_h[which], halo.astype(BF16), NT)
        sides = [side[:, n * width : (n + 1) * width] for n in range(len(some_tiles))]
        area = dot(jnp.concatenate([jnp.concatenate(split(v), axis=1) for v in sides], axis=0), outer[which])
        return {
            (l, t): part[l, span(t), :] + area[n * TILE : (n + 1) * TILE, l * cols : (l + 1) * cols]
            for n, t in enumerate(some_tiles)
            for l in range(layers)
        }


    @pl.when(jnp.logical_not(has_above))
    def _():
        z[top] = jnp.zeros((rows, cols), F32)

    for load in loads[2:]:
        load.wait()
    everywhere = [(l, t, (l, span(t), slice(None))) for t in order for l in range(layers)]
    for l, t, at in everywhere:
        level = (capc[at] + 1).astype(F32) * (1.0 / CAP_LEVELS)
        cap[at] = jnp.where(blocked[at] == 1, 0.0, level)

    def fold(value):
        return jnp.sum((value * value).reshape(TILE // 8, 8, cols), axis=0)

    def sums_begin(step, primal_sum, dual_sum):
        slots[step, pl.ds(me, 1)] = jnp.concatenate(
            [jnp.sum(primal_sum, axis=0, keepdims=True), jnp.sum(dual_sum, axis=0, keepdims=True)],
            axis=0,
        )[None]

        def send(device):
            pltpu.make_async_remote_copy(
                src_ref=slots.at[step, me], dst_ref=slots.at[step, me],
                send_sem=sum_sem.at[0, step], recv_sem=sum_sem.at[1, step],
                device_id=device, device_id_type=MESH,
            ).start()

        ahead(send)

    def sums_end(step, weight):
        some = slots.at[step, pl.ds(0, ndev - 1)]
        pltpu.make_async_copy(some, some, sum_sem.at[1, step]).wait()
        pltpu.make_async_copy(some, some, sum_sem.at[0, step]).wait()
        both = jnp.sum(slots[step], axis=0)
        primal = jnp.sum(both[0:1], axis=1, keepdims=True)
        dual = jnp.sum(both[1:2], axis=1, keepdims=True)
        ratio = jnp.broadcast_to((dual + tiny_term) / (primal + tiny_term), (1, cols))
        return jnp.sqrt(weight) * jnp.sqrt(jnp.sqrt(ratio))

    finish = None
    weight = jnp.ones((1, cols), F32)
    for step in range(ITERS):
        last = step == ITERS - 1
        now = step % 2

        box_early(1, 1)
        for (l, t), area in box_late(ht_y, 1, order).items():
            at = (l, span(t), slice(None))
            grad[at] = cost[at] + area * inverse_area
        if step > 0:
            finish(0)
            weight = sums_end(step - 1, weight)
        tau = step_eta / weight
        sigma = step_eta * weight
        sigma_inverse = 1.0 / sigma

        finish_before = finish
        primal_sum = jnp.zeros((8, cols), F32)
        groups = [g for g in (ends, rest) if g]
        if step == 0:
            blocks = [(range(1, layers), g) for g in groups] + [(range(1), [t]) for t in order]
        else:
            blocks = [(range(layers), g) for g in groups]
        if step == 0:
            hear(0)
        for some_layers, some_tiles in blocks:
            if step == 0 and 0 in some_layers:
                for t in some_tiles:
                    pl.when(has_below)(lambda t=t: first_up(t).wait_recv())
            if step > 0 and (some_layers, some_tiles) == blocks[-1]:
                finish_before(1)
            for t in some_tiles:
                for l in some_layers:
                    at = (l, span(t), slice(None))
                    earlier = zlow[span(t), :] if l == 0 else z[l - 1, span(t), :]
                    slope = grad[at] + (z[at] - earlier)
                    old = x[at]
                    new = jnp.minimum(jnp.maximum(old - tau * slope, 0.0), cap[at])
                    moved = new - old
                    x[at] = new
                    primal_sum = primal_sum + fold(moved)
                    value = new + moved + dens[at]
                    ext_u[l, span(t, HALO), :] = value
                    put_edges(0, l, t, value)
            first_layer = some_layers[0]
            some = pl.ds(first_layer, len(some_layers))
            corner_ready = 0 in some_layers and ends[-1] in some_tiles
            if corner_ready:
                put_corners(
                    ct_u,
                    [ext_u[l, span(0, HALO), :] for l in range(layers)],
                    [ext_u[l, span(tiles - 1, HALO), :] for l in range(layers)],
                )
            if 0 in some_layers:

                @pl.when(has_below)
                def _(step=step, some_tiles=some_tiles):
                    for t in some_tiles:
                        if t in lower:
                            down(step, t).start()

            if top in some_layers:
                going = [t for t in some_tiles if t in upper]

                @pl.when(has_above)
                def _(step=step, going=going):
                    for t in going:
                        up(step, t).start()

            begin(0, SIDE, some, some_tiles, (some_layers, some_tiles) == blocks[-1])
            if ends[-1] in some_tiles:
                begin(0, ROWS, some)
            if corner_ready:
                begin(0, CORNER, every)
            if step == 0:
                if (some_layers, some_tiles) == blocks[1]:
                    hear(1)
        departed(1)
        if step == 0:

            pl.when(has_above)(pltpu.make_async_copy(zlow, zlow, first_sem.at[tiles]).wait)

        dual_sum = jnp.zeros((8, cols), F32)

        def update(old, here, later, keep, sigma=sigma, sigma_inverse=sigma_inverse):
            term = old * sigma_inverse + keep * (here - later)
            return sigma * (term - jnp.clip(term, -layer_gap, layer_gap)) * keep

        for l in range(top):
            for t in order:
                at = (l, span(t), slice(None))
                old = z[at]
                new = update(old, ext_u[l, span(t, HALO), :], ext_u[l + 1, span(t, HALO), :], 1.0)
                z[at] = new
                dual_sum = dual_sum + fold(new - old)

        def other_half(n, last=last, step=step):
            @pl.when(has_below)
            def _():
                for t in upper[n::2]:
                    down(step, t).start()

            if not last:

                @pl.when(has_above)
                def _():
                    for t in lower[n::2]:
                        up(step, t).start()

        box_early(0, 0)
        other_half(0)
        if step == 0:
            hear(2)
        areas = {}
        for t in order:
            if t == ends[0]:
                areas |= box_late(ht_u, 0, ends)
            if rest and t == rest[0]:
                areas |= box_late(ht_u, 0, rest)
            if not last and rest and t == rest[0]:
                put_corners(
                    ct_y,
                    [ext_y[l, span(0, HALO), :] for l in range(layers)],
                    [ext_y[l, span(tiles - 1, HALO), :] for l in range(layers)],
                )
                begin(1, SIDE, every, ends)
                begin(1, ROWS + CORNER, every)
            for l in range(layers):
                area = areas[l, t]
                at = (l, span(t), slice(None))
                old = ext_y[l, span(t, HALO), :]
                term = old * sigma_inverse + area * inverse_area
                capped = jnp.minimum(term, high_density)
                clipped = jnp.where(blocked[at] == 0, jnp.maximum(capped, low_density), capped)
                new = sigma * (term - clipped)
                dual_sum = dual_sum + fold(new - old)
                if last:
                    y_out[at] = new
                else:
                    ext_y[l, span(t, HALO), :] = new
                    put_edges(1, l, t, new)

        if not last:
            begin(1, SIDE, every, rest, True)

        def update_top(t, now=now, update=update):
            at = (top, span(t), slice(None))
            old = z[at]
            new = update(old, ext_u[top, span(t, HALO), :], above[now, span(t), :], keep_top)
            z[at] = new
            return fold(new - old)

        def update_low(t, now=now, update=update):
            old = zlow[span(t), :]
            new = update(old, below[now, span(t), :], ext_u[0, span(t, HALO), :], keep_low)
            zlow[span(t), :] = new
            return fold(new - old)

        def landed(downs, ups, now=now):
            for there, plane, way, some in (
                (has_above, above, 1, downs), (has_below, below, 0, ups)
            ):
                if some:
                    all_of = plane.at[now, pl.ds(0, len(some) * TILE), :]
                    which = portion(some[0], way)
                    pl.when(there)(
                        pltpu.make_async_copy(all_of, all_of, zrecv.at[now, way, which]).wait
                    )

        landed(lower, upper)
        for t in lower:
            dual_sum = dual_sum + update_top(t)
        for t in upper:
            dual_sum = dual_sum + update_low(t)
        if step == 0:
            for n in range(3, rounds):
                hear(n)
        sums_begin(step, primal_sum, dual_sum)
        other_half(1)

        def finish(n, last=last, step=step, now=now, landed=landed,
                   update_top=update_top, update_low=update_low):
            if n == 0:
                for there, way, gone in (
                    (has_below, 1, order), (has_above, 0, upper if last else order)
                ):
                    all_of = above.at[now, pl.ds(0, len(gone) * TILE), :]
                    pl.when(there)(pltpu.make_async_copy(all_of, all_of, zsend.at[now, way]).wait)
                departed(0)
            landed(upper[n::2], [] if last else lower[n::2])
            for t in upper[n::2]:
                update_top(t)
            if not last:
                for t in lower[n::2]:
                    update_low(t)

    finish(0)
    finish(1)
    weight_out[...] = sums_end(ITERS - 1, weight)


def flush(*refs):
    count = len(refs) // 2
    ins, outs, sem = refs[:count], refs[count : 2 * count], refs[2 * count]
    moves = [
        pltpu.make_async_copy(a.at[l, some], b.at[l, some], sem.at[n])
        for n, (a, b) in enumerate(zip(ins, outs))
        for l in range(a.shape[0])
        for some in (pl.ds(0, a.shape[1] // 2), pl.ds(a.shape[1] // 2, a.shape[1] // 2))
    ]
    for move in moves:
        move.start()
    for n, (a, b) in enumerate(zip(ins, outs)):
        pltpu.make_async_copy(a, b, sem.at[n]).wait()


def local(sizes, *args):
    layers, rows, cols = args[0].shape
    ndev = sizes[0] * sizes[1] * sizes[2]
    tiles = rows // TILE
    vmem = pl.BlockSpec(memory_space=pltpu.VMEM)
    anywhere = pl.BlockSpec(memory_space=pl.ANY)
    full = pltpu.VMEM((layers, rows, cols), F32)
    fields = pltpu.VMEM((2, layers, rows, cols), F32)
    field_flags = pltpu.VMEM((2, layers, rows, cols), jnp.int32)
    line = pltpu.VMEM((1, cols), F32)
    ext = pltpu.VMEM((layers, rows + 2 * HALO, cols), F32)
    et = pltpu.VMEM((layers, 2 * HALO, rows), F32)
    ht = pltpu.VMEM((layers, 2 * HALO, rows + 2 * TILE), F32)
    ct = pltpu.VMEM((2, 2, 2 * HALO, TILE), F32)
    ex = pltpu.VMEM((2, layers, rows), F32)
    plane = pltpu.VMEM((rows, cols), F32)
    planes = pltpu.VMEM((2, rows, cols), F32)
    x, y, z, weight = pl.pallas_call(
        functools.partial(kernel, sizes),
        out_shape=(full, full, full, line),
        in_specs=[anywhere] * 7,
        out_specs=(vmem,) * 4,
        scratch_shapes=[
            fields, field_flags,
            ext, ext, et, et, ht, ht, ct, ct, ex, ex, planes, planes, plane, full, full, full,
            pltpu.VMEM((2, TILE, TILE + 2 * HALO), BF16),
            pltpu.VMEM((2, TILE, 3 * TILE), BF16),
            pltpu.VMEM((2, 2 * cols, cols), BF16),
            pltpu.VMEM((2, 2 * layers * 2 * HALO, layers * cols), BF16),
            pltpu.VMEM((2 * HALO, cols), BF16),
            pltpu.VMEM((ITERS, ndev, 2, cols), F32),
            pltpu.SemaphoreType.DMA((5,)),
            pltpu.SemaphoreType.DMA((2, 8)),
            pltpu.SemaphoreType.DMA((2, 8)),
            pltpu.SemaphoreType.DMA((tiles + 1,)),
            pltpu.SemaphoreType.DMA((2, 2)),
            pltpu.SemaphoreType.DMA((2, 2, 3)),
            pltpu.SemaphoreType.DMA((2, ITERS)),
            pltpu.SemaphoreType.REGULAR((len(spreads(sizes)) + 2,)),
        ],
        compiler_params=pltpu.CompilerParams(collective_id=0, has_side_effects=True),
        name="fill_steps",
    )(*args)
    whole = jax.ShapeDtypeStruct((layers, rows, cols), F32)
    x, y, z = pl.pallas_call(
        flush,
        out_shape=(whole,) * 3,
        in_specs=[anywhere] * 3,
        out_specs=(anywhere,) * 3,
        scratch_shapes=[pltpu.SemaphoreType.DMA((3,))],
        name="flush",
    )(*(pltpu.with_memory_space_constraint(value, pltpu.VMEM) for value in (x, y, z)))
    return x, y, z, weight[0, 0]


def solution(mesh):
    sizes = tuple(mesh.shape[axis] for axis in ("layer", "row", "col"))
    spec = P("layer", "row", "col")
    return jax.shard_map(
        functools.partial(local, sizes),
        mesh=mesh,
        in_specs=(spec,) * 7,
        out_specs=(spec, spec, spec, P()),
        check_vma=False,
    )
```

```python
import functools

import jax
import jax.numpy as jnp
from jax import lax
from jax.experimental import pallas as pl
from jax.experimental.pallas import tpu as pltpu
from jax.sharding import PartitionSpec as P

WIN = 50
CAP_LEVELS = 8
ITERS = 3

step_eta = 0.4
low_density = 0.35
high_density = 0.65
layer_gap = 0.15
tiny_term = 1e-06

HALF = WIN // 2
HALO = -(-HALF // 16) * 16
MOST = (HALF - 1) // 8 * 8
assert WIN == 2 * HALF and MOST == HALF - 1
TILE = 128
MESH = pl.DeviceIdType.MESH
HBM, EXTRA = "hbm", "extra"
DIRS = ((-1, 0), (1, 0), (0, -1), (0, 1), (-1, -1), (-1, 1), (1, -1), (1, 1))
ROWS = (0, 1)
SIDE = (2, 3)
CORNER = (4, 5, 6, 7)
F32 = jnp.float32
BF16 = jnp.bfloat16
NT = (((1,), (1,)), ((), ()))
NN = (((1,), (0,)), ((), ()))


def split(value):
    high = value.astype(BF16)
    low = (value - high.astype(F32)).astype(BF16)
    return high, low


def dot(left, right, dims=NN):
    return lax.dot_general(left, right, dims, preferred_element_type=F32)


def iota(shape, dim):
    return lax.broadcasted_iota(jnp.int32, shape, dim)


def window(offset, start):
    return jnp.where((offset >= start) & (offset < start + WIN), 1.0, 0.0).astype(BF16)


def spreads(sizes):
    distance, result = 1, []
    while distance < max(sizes) - 1:
        result.append(distance)
        distance *= 2
    return result


def kernel(
    sizes, cost_in, dens_in, capc_in, blocked_in, x_in, y_in, z_in,
    x, y_out, z, weight_out,
    reals, flags,
    ext_u, ext_y, et_u, et_y, ht_u, ht_y, ct_u, ct_y, ex_u, ex_y, above, below, zlow, cap, grad, part,
    band_r, band_h, inner, outer, pick, slots,
    load_sem, send_sem, recv_sem, first_sem, zsend, zrecv, sum_sem, ready,
):
    nl, nr, nc = sizes
    layers, rows, cols = x_in.shape
    top = layers - 1
    ndev = nl * nr * nc
    il, ir, ic = lax.axis_index("layer"), lax.axis_index("row"), lax.axis_index("col")
    me = (il * nr + ir) * nc + ic
    cost, dens, capc, blocked = reals.at[0], reals.at[1], flags.at[0], flags.at[1]
    tiles = rows // TILE
    order = list(dict.fromkeys((0, tiles - 1, *range(tiles))))
    ends = order[:2]
    rest = order[2:]
    inverse_area = 1.0 / (WIN * WIN)
    own = pl.ds(HALO, rows)
    has_above, has_below = il < nl - 1, il > 0

    pairs = (
        (y_in, ext_y.at[:, own, :], 0), (z_in, z, 1), (cost_in, cost, 2), (dens_in, dens, 2),
        (x_in, x, 3), (capc_in, capc, 4), (blocked_in, blocked, 4),
    )
    loads = [
        pltpu.make_async_copy(ref, ref, load_sem.at[n])
        for n, ref in enumerate((ext_y.at[:, own, :], z, reals, x, flags))
    ]

    for ref in (ext_u, ext_y):
        ref[:, :HALO, :] = jnp.zeros((layers, HALO, cols), F32)
        ref[:, HALO + rows :, :] = jnp.zeros((layers, HALO, cols), F32)
    for ref in (ht_u, ht_y, ct_u, ct_y, ex_u, ex_y):
        ref[...] = jnp.zeros(ref.shape, F32)

    barrier = pltpu.get_barrier_semaphore()

    def ahead(act):
        def one(k, _):
            i = lax.rem(me + k, ndev)
            act((i // (nr * nc), (i // nc) % nr, i % nc))
            return 0

        lax.fori_loop(1, ndev, one, 0, unroll=ndev <= 32)

    def lines(act):
        for n in range(1, nl):
            act((lax.rem(il + n, nl), ir, ic))
        for n in range(1, nr):
            act((il, lax.rem(ir + n, nr), ic))
        for n in range(1, nc):
            act((il, ir, lax.rem(ic + n, nc)))

    def beside(distance):
        peers = []
        for axis, (at, n) in enumerate(((il, nl), (ir, nr), (ic, nc))):
            if distance < n:
                for there, to in ((at >= distance, at - distance), (at < n - distance, at + distance)):
                    device = [il, ir, ic]
                    device[axis] = to
                    peers.append((there, tuple(device)))
        return peers

    line_peers = nl + nr + nc - 3
    corners = []
    for dr, dc in DIRS[4:]:
        there = jnp.logical_and(
            ir < nr - 1 if dr > 0 else ir > 0, ic < nc - 1 if dc > 0 else ic > 0
        )
        corners.append((there, (il, ir + dr, ic + dc)))

    def signal(semaphore, device):
        pl.semaphore_signal(semaphore, inc=1, device_id=device, device_id_type=MESH)

    def signal_some(semaphore, peers):
        for there, device in peers:
            pl.when(there)(functools.partial(signal, semaphore, device))

    def wait_some(semaphore, peers):
        pl.semaphore_wait(semaphore, sum(there.astype(jnp.int32) for there, _ in peers))

    signal_some(barrier, beside(1) + corners)
    for a, b, n in pairs:
        pltpu.make_async_copy(a, b, load_sem.at[n]).start()

    @pl.when(jnp.logical_not(has_above))
    def _():
        above[...] = jnp.zeros(above.shape, F32)

    @pl.when(jnp.logical_not(has_below))
    def _():
        below[...] = jnp.zeros(below.shape, F32)
        zlow[...] = jnp.zeros(zlow.shape, F32)

    spread = spreads(sizes)
    rounds = len(spread) + 2

    def tell(n):
        if n < len(spread):
            signal_some(ready.at[n], beside(spread[n]))
        elif n < rounds:
            lines(functools.partial(signal, ready.at[n]))

    def hear(n):
        if n < len(spread):
            wait_some(ready.at[n], beside(spread[n]))
        elif n < rounds:
            pl.semaphore_wait(ready.at[n], line_peers)
        tell(n + 1)

    def span(t, base=0):
        return pl.ds(t * TILE + base, TILE)

    wait_some(barrier, beside(1) + corners)

    def first_up(t):
        return pltpu.make_async_remote_copy(
            src_ref=z.at[top, span(t), :], dst_ref=zlow.at[span(t), :],
            send_sem=first_sem.at[tiles], recv_sem=first_sem.at[t],
            device_id=(il + 1, ir, ic), device_id_type=MESH,
        )

    loads[1].wait()

    @pl.when(has_above)
    def _():
        for t in order:
            first_up(t).start()


    tell(0)

    keep_top = jnp.where(has_above, 1.0, 0.0).astype(F32)
    keep_low = jnp.where(has_below, 1.0, 0.0).astype(F32)
    shape = (2 * HALO, cols)
    k = iota(shape, 0)
    place = jnp.where(k < HALO, k, k - 2 * HALO + cols)
    pick[...] = jnp.where(place == iota(shape, 1), 1.0, 0.0).astype(BF16)

    def put_edges(field, l, t, value):
        et, ex = ((et_u, ex_u), (et_y, ex_y))[field]
        turned = value.T
        beyond = cols - HALF if field == 0 else HALF - 1
        ex[0, l : l + 1, span(t)] = turned[beyond : beyond + 1]
        et[l, :HALO, span(t)] = turned[:HALO]
        et[l, HALO:, span(t)] = turned[cols - HALO :]

    def put_corners(ct, first, final):
        blank = jnp.zeros((TILE - layers * HALO, cols), F32)
        for n, pieces in enumerate(
            ([value[:HALO] for value in first], [value[TILE - HALO :] for value in final])
        ):
            ct[0, n] = dot(pick[...], jnp.concatenate(pieces + [blank], axis=0).astype(BF16), NT)

    def take_corners(ct, ht):
        for l in range(layers):
            ht[l, :, :TILE] = pltpu.roll(ct[1, 1], TILE - (l + 1) * HALO, axis=1)
            last_tile = ct[1, 0]
            ht[l, :, TILE + rows :] = pltpu.roll(last_tile, TILE - l * HALO, axis=1) if l else last_tile

    def copies(field):
        ext, et, ht, ct, ex = (
            (ext_u, et_u, ht_u, ct_u, ex_u), (ext_y, et_y, ht_y, ct_y, ex_y)
        )[field]
        longer = 1 if field == 0 else -1
        result = []
        for d, (dr, dc) in enumerate(DIRS):
            wide = HALO if dr and dc == longer else MOST
            from_rows = pl.ds(0 if dc < 0 else 2 * HALO - wide, wide)
            to_rows = pl.ds(HALO if dc < 0 else HALO - wide, wide)
            tall = HALO if dr == longer else MOST

            def ends_of(some, t, dr=dr, dc=dc, from_rows=from_rows, to_rows=to_rows, tall=tall):
                if dc == 0:
                    return (
                        y_in.at[some, pl.ds(0 if dr < 0 else rows - tall, tall), :] if t is HBM
                        else ext.at[some, pl.ds(HALO if dr < 0 else HALO + rows - tall, tall), :],
                        ext.at[some, pl.ds(HALO + rows if dr < 0 else HALO - tall, tall), :],
                    )
                if dr == 0:
                    if t is EXTRA:
                        return ex.at[0], ex.at[1]
                    if t is None:
                        return et.at[some, from_rows, :], ht.at[some, to_rows, pl.ds(TILE, rows)]
                    return et.at[some, from_rows, span(t)], ht.at[some, to_rows, span(t, TILE)]
                n = 0 if dr < 0 else 1
                return ct.at[0, n, from_rows, :], ct.at[1, n, to_rows, :]

            def make(some, t=None, d=d, dr=dr, dc=dc, ends_of=ends_of):
                src, dst = ends_of(some, t)
                return pltpu.make_async_remote_copy(
                    src_ref=src, dst_ref=dst, send_sem=send_sem.at[field, d],
                    recv_sem=recv_sem.at[field, d],
                    device_id=(il, ir + dr, ic + dc), device_id_type=MESH,
                )

            to, frm = [], []
            if dr < 0:
                to.append(ir > 0)
                frm.append(ir < nr - 1)
            if dr > 0:
                to.append(ir < nr - 1)
                frm.append(ir > 0)
            if dc < 0:
                to.append(ic > 0)
                frm.append(ic < nc - 1)
            if dc > 0:
                to.append(ic < nc - 1)
                frm.append(ic > 0)

            def both(semaphore, d=d):
                size = above.at[0, pl.ds(0, layers * HALF * rows // cols), :]
                return pltpu.make_async_copy(size, size, semaphore.at[field, d])

            if dr or dc != longer:
                both = None

            result.append(
                (make, both, functools.reduce(jnp.logical_and, to), functools.reduce(jnp.logical_and, frm))
            )
        return result

    halo_copies = (copies(0), copies(1))
    every = slice(None)

    def begin(field, which, some, some_tiles=(None,), whole=False):
        for d in which:
            make, both, to, _ = halo_copies[field][d]

            @pl.when(to)
            def _(make=make, both=both):
                for t in some_tiles:
                    make(some, t).start()
                if whole and both:
                    make(every, EXTRA).start()

    def arrived(field, which):
        for d in which:
            make, both, _, frm = halo_copies[field][d]
            pl.when(frm)(
                lambda make=make, both=both: (both(recv_sem).wait() if both else make(every).wait_recv())
            )

    def departed(field):
        for make, both, to, _ in halo_copies[field]:
            pl.when(to)(
                lambda make=make, both=both: (both(send_sem).wait() if both else make(every).wait_send())
            )

    begin(1, ROWS, every, (HBM,))
    loads[0].wait()
    for t in range(tiles):
        for l in range(layers):
            put_edges(1, l, t, ext_y[l, span(t, HALO), :])
    put_corners(
        ct_y,
        [ext_y[l, span(0, HALO), :] for l in range(layers)],
        [ext_y[l, span(tiles - 1, HALO), :] for l in range(layers)],
    )
    begin(1, SIDE + CORNER, every, whole=True)

    lower, upper = order[::2], order[1::2]

    def portion(t, way):
        if t in (upper, lower)[way]:
            return 0
        return 1 + (lower, upper)[way].index(t) % 2

    def up(step, t):
        side = step % 2
        return pltpu.make_async_remote_copy(
            src_ref=ext_u.at[top, span(t, HALO), :], dst_ref=below.at[side, span(t), :],
            send_sem=zsend.at[side, 0], recv_sem=zrecv.at[side, 0, portion(t, 0)],
            device_id=(il + 1, ir, ic), device_id_type=MESH,
        )

    def down(step, t):
        side = step % 2
        return pltpu.make_async_remote_copy(
            src_ref=ext_u.at[0, span(t, HALO), :], dst_ref=above.at[side, span(t), :],
            send_sem=zsend.at[side, 1], recv_sem=zrecv.at[side, 1, portion(t, 1)],
            device_id=(il - 1, ir, ic), device_id_type=MESH,
        )

    width = layers * 2 * HALO
    for which, start in ((0, -HALF), (1, 1 - HALF)):
        shape = (TILE, TILE + 2 * HALO)
        band_r[which] = window(iota(shape, 1) - HALO - iota(shape, 0), start)
        shape = (TILE, 3 * TILE)
        band_h[which] = window(iota(shape, 1) - TILE - iota(shape, 0), start)
        shape = (cols, cols)
        own_cols = window(iota(shape, 0) - iota(shape, 1), start)
        shape = (2 * HALO, cols)
        k = iota(shape, 0)
        place = jnp.where(k < HALO, k - HALO, k - HALO + cols)
        halo_cols = window(place - iota(shape, 1), start)
        blank = jnp.zeros(shape, BF16)
        for n in range(2):
            inner[which, n * cols : (n + 1) * cols] = own_cols
            for m in range(layers):
                at = n * width + m * 2 * HALO
                for l in range(layers):
                    outer[which, at : at + 2 * HALO, l * cols : (l + 1) * cols] = (
                        halo_cols if m == l else blank
                    )

    def box_own(ext, which, some_tiles):
        pieces = []
        for t in some_tiles:
            tall = pl.ds(t * TILE, TILE + 2 * HALO)
            wide = jnp.concatenate([ext[l, tall, :].astype(BF16) for l in range(layers)], axis=1)
            mid = dot(band_r[which], wide)
            pieces += [
                jnp.concatenate(split(mid[:, l * cols : (l + 1) * cols]), axis=1)
                for l in range(layers)
            ]
        area = dot(jnp.concatenate(pieces, axis=0), inner[which])
        for n, t in enumerate(some_tiles):
            for l in range(layers):
                at = (n * layers + l) * TILE
                part[l, span(t), :] = area[at : at + TILE]

    def box_early(field, which):
        ext = (ext_u, ext_y)[field]
        if rest:
            box_own(ext, which, rest)
        arrived(field, ROWS)
        box_own(ext, which, ends)
        arrived(field, CORNER + SIDE)
        ht, ex = ((ht_u, ex_u), (ht_y, ex_y))[field]
        take_corners((ct_u, ct_y)[field], ht)
        row = HALO - HALF if field == 0 else HALO + HALF - 1
        for l in range(layers):
            ht[l, row : row + 1, TILE : TILE + rows] = ex[1, l : l + 1]

    def box_late(ht, which, some_tiles):
        halo = jnp.concatenate(
            [ht[:, :, t * TILE : (t + 3) * TILE].reshape(width, 3 * TILE) for t in some_tiles], axis=0
        )
        side = dot(band_h[which], halo.astype(BF16), NT)
        sides = [side[:, n * width : (n + 1) * width] for n in range(len(some_tiles))]
        area = dot(jnp.concatenate([jnp.concatenate(split(v), axis=1) for v in sides], axis=0), outer[which])
        return {
            (l, t): part[l, span(t), :] + area[n * TILE : (n + 1) * TILE, l * cols : (l + 1) * cols]
            for n, t in enumerate(some_tiles)
            for l in range(layers)
        }


    @pl.when(jnp.logical_not(has_above))
    def _():
        z[top] = jnp.zeros((rows, cols), F32)

    for load in loads[2:]:
        load.wait()
    everywhere = [(l, t, (l, span(t), slice(None))) for t in order for l in range(layers)]
    for l, t, at in everywhere:
        level = (capc[at] + 1).astype(F32) * (1.0 / CAP_LEVELS)
        cap[at] = jnp.where(blocked[at] == 1, 0.0, level)

    def fold(value):
        return jnp.sum((value * value).reshape(TILE // 8, 8, cols), axis=0)

    def sums_begin(step, primal_sum, dual_sum):
        left = iota((8, cols), 1) < cols // 2
        both = jnp.where(left, primal_sum, dual_sum)
        across = pltpu.roll(jnp.where(left, dual_sum, primal_sum), cols // 2, axis=1)
        slots[step, pl.ds(me, 1)] = jnp.sum(both + across, axis=0, keepdims=True)[None]

        def send(device):
            pltpu.make_async_remote_copy(
                src_ref=slots.at[step, me], dst_ref=slots.at[step, me],
                send_sem=sum_sem.at[ITERS], recv_sem=sum_sem.at[step],
                device_id=device, device_id_type=MESH,
            ).start()

        ahead(send)

    def sums_end(step, weight):
        some = slots.at[step, pl.ds(0, ndev - 1)]
        pltpu.make_async_copy(some, some, sum_sem.at[step]).wait()
        both = jnp.sum(slots[step], axis=0)
        left = iota((1, cols), 1) < cols // 2
        primal = jnp.sum(jnp.where(left, both, 0.0), axis=1, keepdims=True)
        dual = jnp.sum(jnp.where(left, 0.0, both), axis=1, keepdims=True)
        ratio = jnp.broadcast_to((dual + tiny_term) / (primal + tiny_term), (1, cols))
        return jnp.sqrt(weight) * jnp.sqrt(jnp.sqrt(ratio))

    finish = None
    weight = jnp.ones((1, cols), F32)
    for step in range(ITERS):
        last = step == ITERS - 1
        now = step % 2

        box_early(1, 1)
        for (l, t), area in box_late(ht_y, 1, order).items():
            at = (l, span(t), slice(None))
            grad[at] = cost[at] + area * inverse_area
        if step > 0:
            finish(0)
            weight = sums_end(step - 1, weight)
        tau = step_eta / weight
        sigma = step_eta * weight
        sigma_inverse = 1.0 / sigma

        finish_before = finish
        primal_sum = jnp.zeros((8, cols), F32)
        groups = [g for g in (ends[:1], ends[1:], rest) if g]
        if step == 0:
            blocks = [(range(1, layers), g) for g in groups] + [(range(1), [t]) for t in order]
        else:
            blocks = [(range(layers), g) for g in groups]
        if step == 0:
            hear(0)
        for some_layers, some_tiles in blocks:
            if step == 0 and 0 in some_layers:
                for t in some_tiles:
                    pl.when(has_below)(lambda t=t: first_up(t).wait_recv())
            if step > 0 and (some_layers, some_tiles) == blocks[-1]:
                finish_before(1)
            for t in some_tiles:
                for l in some_layers:
                    at = (l, span(t), slice(None))
                    earlier = zlow[span(t), :] if l == 0 else z[l - 1, span(t), :]
                    slope = grad[at] + (z[at] - earlier)
                    old = x[at]
                    new = jnp.minimum(jnp.maximum(old - tau * slope, 0.0), cap[at])
                    moved = new - old
                    x[at] = new
                    primal_sum = primal_sum + fold(moved)
                    value = new + moved + dens[at]
                    ext_u[l, span(t, HALO), :] = value
                    put_edges(0, l, t, value)
            first_layer = some_layers[0]
            some = pl.ds(first_layer, len(some_layers))
            corner_ready = 0 in some_layers and ends[-1] in some_tiles
            if corner_ready:
                put_corners(
                    ct_u,
                    [ext_u[l, span(0, HALO), :] for l in range(layers)],
                    [ext_u[l, span(tiles - 1, HALO), :] for l in range(layers)],
                )
            if 0 in some_layers:

                @pl.when(has_below)
                def _(step=step, some_tiles=some_tiles):
                    for t in some_tiles:
                        if t in lower:
                            down(step, t).start()

            if top in some_layers:
                going = [t for t in some_tiles if t in upper]

                @pl.when(has_above)
                def _(step=step, going=going):
                    for t in going:
                        up(step, t).start()

            begin(0, SIDE, some, some_tiles, (some_layers, some_tiles) == blocks[-1])
            if ends[-1] in some_tiles:
                begin(0, ROWS, some)
            if corner_ready:
                begin(0, CORNER, every)
            if step == 0:
                if (some_layers, some_tiles) == blocks[1]:
                    hear(1)
        departed(1)
        if step == 0:

            pl.when(has_above)(pltpu.make_async_copy(zlow, zlow, first_sem.at[tiles]).wait)

        dual_sum = jnp.zeros((8, cols), F32)

        def update(old, here, later, keep, sigma=sigma, sigma_inverse=sigma_inverse):
            term = old * sigma_inverse + keep * (here - later)
            return sigma * (term - jnp.clip(term, -layer_gap, layer_gap)) * keep

        for l in range(top):
            for t in order:
                at = (l, span(t), slice(None))
                old = z[at]
                new = update(old, ext_u[l, span(t, HALO), :], ext_u[l + 1, span(t, HALO), :], 1.0)
                z[at] = new
                dual_sum = dual_sum + fold(new - old)

        def other_half(n, last=last, step=step):
            @pl.when(has_below)
            def _():
                for t in upper[n::2]:
                    down(step, t).start()

            if not last:

                @pl.when(has_above)
                def _():
                    for t in lower[n::2]:
                        up(step, t).start()

        box_early(0, 0)
        other_half(0)
        if step == 0:
            hear(2)
        areas = {}
        for t in order:
            if t == ends[0]:
                areas |= box_late(ht_u, 0, ends)
            if rest and t == rest[0]:
                areas |= box_late(ht_u, 0, rest)
            if not last and rest and t == rest[0]:
                put_corners(
                    ct_y,
                    [ext_y[l, span(0, HALO), :] for l in range(layers)],
                    [ext_y[l, span(tiles - 1, HALO), :] for l in range(layers)],
                )
                begin(1, SIDE, every, ends)
                begin(1, ROWS + CORNER, every)
            for l in range(layers):
                area = areas[l, t]
                at = (l, span(t), slice(None))
                old = ext_y[l, span(t, HALO), :]
                term = old * sigma_inverse + area * inverse_area
                capped = jnp.minimum(term, high_density)
                clipped = jnp.where(blocked[at] == 0, jnp.maximum(capped, low_density), capped)
                new = sigma * (term - clipped)
                dual_sum = dual_sum + fold(new - old)
                if last:
                    y_out[at] = new
                else:
                    ext_y[l, span(t, HALO), :] = new
                    put_edges(1, l, t, new)

        if not last:
            begin(1, SIDE, every, rest, True)

        def update_top(t, now=now, update=update):
            at = (top, span(t), slice(None))
            old = z[at]
            new = update(old, ext_u[top, span(t, HALO), :], above[now, span(t), :], keep_top)
            z[at] = new
            return fold(new - old)

        def update_low(t, now=now, update=update):
            old = zlow[span(t), :]
            new = update(old, below[now, span(t), :], ext_u[0, span(t, HALO), :], keep_low)
            zlow[span(t), :] = new
            return fold(new - old)

        def landed(downs, ups, now=now):
            for there, plane, way, some in (
                (has_above, above, 1, downs), (has_below, below, 0, ups)
            ):
                if some:
                    all_of = plane.at[now, pl.ds(0, len(some) * TILE), :]
                    which = portion(some[0], way)
                    pl.when(there)(
                        pltpu.make_async_copy(all_of, all_of, zrecv.at[now, way, which]).wait
                    )

        landed(lower, upper)
        for t in lower:
            dual_sum = dual_sum + update_top(t)
        for t in upper:
            dual_sum = dual_sum + update_low(t)
        if step == 0:
            for n in range(3, rounds):
                hear(n)
        sums_begin(step, primal_sum, dual_sum)
        other_half(1)

        def finish(n, last=last, step=step, now=now, landed=landed,
                   update_top=update_top, update_low=update_low):
            if n == 0:
                for there, way, gone in (
                    (has_below, 1, order), (has_above, 0, upper if last else order)
                ):
                    all_of = above.at[now, pl.ds(0, len(gone) * TILE), :]
                    pl.when(there)(pltpu.make_async_copy(all_of, all_of, zsend.at[now, way]).wait)
                departed(0)
            landed(upper[n::2], [] if last else lower[n::2])
            for t in upper[n::2]:
                update_top(t)
            if not last:
                for t in lower[n::2]:
                    update_low(t)

    finish(0)
    finish(1)
    weight_out[...] = sums_end(ITERS - 1, weight)
    gone = slots.at[:, pl.ds(0, ndev - 1)]
    pltpu.make_async_copy(gone, gone, sum_sem.at[ITERS]).wait()


def flush(*refs):
    count = len(refs) // 2
    ins, outs, sem = refs[:count], refs[count : 2 * count], refs[2 * count]
    moves = [
        pltpu.make_async_copy(a.at[l, some], b.at[l, some], sem.at[n])
        for n, (a, b) in enumerate(zip(ins, outs))
        for l in range(a.shape[0])
        for some in (pl.ds(0, a.shape[1] // 2), pl.ds(a.shape[1] // 2, a.shape[1] // 2))
    ]
    for move in moves:
        move.start()
    for n, (a, b) in enumerate(zip(ins, outs)):
        pltpu.make_async_copy(a, b, sem.at[n]).wait()


def local(sizes, *args):
    layers, rows, cols = args[0].shape
    ndev = sizes[0] * sizes[1] * sizes[2]
    tiles = rows // TILE
    vmem = pl.BlockSpec(memory_space=pltpu.VMEM)
    anywhere = pl.BlockSpec(memory_space=pl.ANY)
    full = pltpu.VMEM((layers, rows, cols), F32)
    fields = pltpu.VMEM((2, layers, rows, cols), F32)
    field_flags = pltpu.VMEM((2, layers, rows, cols), jnp.int32)
    line = pltpu.VMEM((1, cols), F32)
    ext = pltpu.VMEM((layers, rows + 2 * HALO, cols), F32)
    et = pltpu.VMEM((layers, 2 * HALO, rows), F32)
    ht = pltpu.VMEM((layers, 2 * HALO, rows + 2 * TILE), F32)
    ct = pltpu.VMEM((2, 2, 2 * HALO, TILE), F32)
    ex = pltpu.VMEM((2, layers, rows), F32)
    plane = pltpu.VMEM((rows, cols), F32)
    planes = pltpu.VMEM((2, rows, cols), F32)
    x, y, z, weight = pl.pallas_call(
        functools.partial(kernel, sizes),
        out_shape=(full, full, full, line),
        in_specs=[anywhere] * 7,
        out_specs=(vmem,) * 4,
        scratch_shapes=[
            fields, field_flags,
            ext, ext, et, et, ht, ht, ct, ct, ex, ex, planes, planes, plane, full, full, full,
            pltpu.VMEM((2, TILE, TILE + 2 * HALO), BF16),
            pltpu.VMEM((2, TILE, 3 * TILE), BF16),
            pltpu.VMEM((2, 2 * cols, cols), BF16),
            pltpu.VMEM((2, 2 * layers * 2 * HALO, layers * cols), BF16),
            pltpu.VMEM((2 * HALO, cols), BF16),
            pltpu.VMEM((ITERS, ndev, 1, cols), F32),
            pltpu.SemaphoreType.DMA((5,)),
            pltpu.SemaphoreType.DMA((2, 8)),
            pltpu.SemaphoreType.DMA((2, 8)),
            pltpu.SemaphoreType.DMA((tiles + 1,)),
            pltpu.SemaphoreType.DMA((2, 2)),
            pltpu.SemaphoreType.DMA((2, 2, 3)),
            pltpu.SemaphoreType.DMA((ITERS + 1,)),
            pltpu.SemaphoreType.REGULAR((len(spreads(sizes)) + 2,)),
        ],
        compiler_params=pltpu.CompilerParams(collective_id=0, has_side_effects=True),
        name="fill_steps",
    )(*args)
    whole = jax.ShapeDtypeStruct((layers, rows, cols), F32)
    x, y, z = pl.pallas_call(
        flush,
        out_shape=(whole,) * 3,
        in_specs=[anywhere] * 3,
        out_specs=(anywhere,) * 3,
        scratch_shapes=[pltpu.SemaphoreType.DMA((3,))],
        name="flush",
    )(*(pltpu.with_memory_space_constraint(value, pltpu.VMEM) for value in (x, y, z)))
    return x, y, z, weight[0, 0]


def solution(mesh):
    sizes = tuple(mesh.shape[axis] for axis in ("layer", "row", "col"))
    spec = P("layer", "row", "col")
    return jax.shard_map(
        functools.partial(local, sizes),
        mesh=mesh,
        in_specs=(spec,) * 7,
        out_specs=(spec, spec, spec, P()),
        check_vma=False,
    )
```

```python
import functools

import jax
import jax.numpy as jnp
from jax import lax
from jax.experimental import pallas as pl
from jax.experimental.pallas import tpu as pltpu
from jax.sharding import PartitionSpec as P

WIN = 50
CAP_LEVELS = 8
ITERS = 3

step_eta = 0.4
low_density = 0.35
high_density = 0.65
layer_gap = 0.15
tiny_term = 1e-06

HALF = WIN // 2
HALO = -(-HALF // 16) * 16
MOST = (HALF - 1) // 8 * 8
assert WIN == 2 * HALF and MOST == HALF - 1
TILE = 128
MESH = pl.DeviceIdType.MESH
HBM, EXTRA = "hbm", "extra"
DIRS = ((-1, 0), (1, 0), (0, -1), (0, 1), (-1, -1), (-1, 1), (1, -1), (1, 1))
ROWS = (0, 1)
SIDE = (2, 3)
CORNER = (4, 5, 6, 7)
F32 = jnp.float32
BF16 = jnp.bfloat16
NT = (((1,), (1,)), ((), ()))
NN = (((1,), (0,)), ((), ()))


def split(value):
    high = value.astype(BF16)
    low = (value - high.astype(F32)).astype(BF16)
    return high, low


def dot(left, right, dims=NN):
    return lax.dot_general(left, right, dims, preferred_element_type=F32)


def iota(shape, dim):
    return lax.broadcasted_iota(jnp.int32, shape, dim)


def window(offset, start):
    return jnp.where((offset >= start) & (offset < start + WIN), 1.0, 0.0).astype(BF16)


def spreads(sizes):
    distance, result = 1, []
    while distance < max(sizes) - 1:
        result.append(distance)
        distance *= 2
    return result


def kernel(
    sizes, cost_in, dens_in, capc_in, blocked_in, x_in, y_in, z_in,
    x, y_out, z, weight_out,
    reals, flags,
    ext_u, ext_y, et_u, et_y, ht_u, ht_y, ct_u, ct_y, ex_u, ex_y, above, below, zlow, cap, grad, part,
    band_r, band_h, inner, outer, pick, slots,
    load_sem, send_sem, recv_sem, first_sem, zsend, zrecv, sum_sem, ready,
):
    nl, nr, nc = sizes
    layers, rows, cols = x_in.shape
    top = layers - 1
    ndev = nl * nr * nc
    il, ir, ic = lax.axis_index("layer"), lax.axis_index("row"), lax.axis_index("col")
    me = (il * nr + ir) * nc + ic
    cost, dens, capc, blocked = reals.at[0], reals.at[1], flags.at[0], flags.at[1]
    tiles = rows // TILE
    order = list(dict.fromkeys((0, tiles - 1, *range(tiles))))
    ends = order[:2]
    rest = order[2:]
    inverse_area = 1.0 / (WIN * WIN)
    own = pl.ds(HALO, rows)
    has_above, has_below = il < nl - 1, il > 0

    pairs = (
        (y_in, ext_y.at[:, own, :], 0), (z_in, z, 1), (cost_in, cost, 2), (dens_in, dens, 2),
        (x_in, x, 3), (capc_in, capc, 4), (blocked_in, blocked, 4),
    )
    loads = [
        pltpu.make_async_copy(ref, ref, load_sem.at[n])
        for n, ref in enumerate((ext_y.at[:, own, :], z, reals, x, flags))
    ]

    for ref in (ext_u, ext_y):
        ref[:, :HALO, :] = jnp.zeros((layers, HALO, cols), F32)
        ref[:, HALO + rows :, :] = jnp.zeros((layers, HALO, cols), F32)
    for ref in (ht_u, ht_y, ct_u, ct_y, ex_u, ex_y):
        ref[...] = jnp.zeros(ref.shape, F32)

    barrier = pltpu.get_barrier_semaphore()

    def ahead(act):
        def one(k, _):
            i = lax.rem(me + k, ndev)
            act((i // (nr * nc), (i // nc) % nr, i % nc))
            return 0

        lax.fori_loop(1, ndev, one, 0, unroll=ndev <= 32)

    def lines(act):
        for n in range(1, nl):
            act((lax.rem(il + n, nl), ir, ic))
        for n in range(1, nr):
            act((il, lax.rem(ir + n, nr), ic))
        for n in range(1, nc):
            act((il, ir, lax.rem(ic + n, nc)))

    def beside(distance):
        peers = []
        for axis, (at, n) in enumerate(((il, nl), (ir, nr), (ic, nc))):
            if distance < n:
                for there, to in ((at >= distance, at - distance), (at < n - distance, at + distance)):
                    device = [il, ir, ic]
                    device[axis] = to
                    peers.append((there, tuple(device)))
        return peers

    line_peers = nl + nr + nc - 3
    corners = []
    for dr, dc in DIRS[4:]:
        there = jnp.logical_and(
            ir < nr - 1 if dr > 0 else ir > 0, ic < nc - 1 if dc > 0 else ic > 0
        )
        corners.append((there, (il, ir + dr, ic + dc)))

    def signal(semaphore, device):
        pl.semaphore_signal(semaphore, inc=1, device_id=device, device_id_type=MESH)

    def signal_some(semaphore, peers):
        for there, device in peers:
            pl.when(there)(functools.partial(signal, semaphore, device))

    def wait_some(semaphore, peers):
        pl.semaphore_wait(semaphore, sum(there.astype(jnp.int32) for there, _ in peers))

    signal_some(barrier, beside(1) + corners)
    for a, b, n in pairs:
        pltpu.make_async_copy(a, b, load_sem.at[n]).start()

    @pl.when(jnp.logical_not(has_above))
    def _():
        above[...] = jnp.zeros(above.shape, F32)

    @pl.when(jnp.logical_not(has_below))
    def _():
        below[...] = jnp.zeros(below.shape, F32)
        zlow[...] = jnp.zeros(zlow.shape, F32)

    spread = spreads(sizes)
    rounds = len(spread) + 2

    def tell(n):
        if n < len(spread):
            signal_some(ready.at[n], beside(spread[n]))
        elif n < rounds:
            lines(functools.partial(signal, ready.at[n]))

    def hear(n):
        if n < len(spread):
            wait_some(ready.at[n], beside(spread[n]))
        elif n < rounds:
            pl.semaphore_wait(ready.at[n], line_peers)
        tell(n + 1)

    def span(t, base=0):
        return pl.ds(t * TILE + base, TILE)

    wait_some(barrier, beside(1) + corners)

    def first_up(t):
        return pltpu.make_async_remote_copy(
            src_ref=z.at[top, span(t), :], dst_ref=zlow.at[span(t), :],
            send_sem=first_sem.at[tiles], recv_sem=first_sem.at[t],
            device_id=(il + 1, ir, ic), device_id_type=MESH,
        )

    loads[1].wait()

    @pl.when(has_above)
    def _():
        for t in order:
            first_up(t).start()


    tell(0)

    keep_top = jnp.where(has_above, 1.0, 0.0).astype(F32)
    keep_low = jnp.where(has_below, 1.0, 0.0).astype(F32)
    shape = (2 * HALO, cols)
    k = iota(shape, 0)
    place = jnp.where(k < HALO, k, k - 2 * HALO + cols)
    pick[...] = jnp.where(place == iota(shape, 1), 1.0, 0.0).astype(BF16)

    def put_edges(field, l, t, value):
        et, ex = ((et_u, ex_u), (et_y, ex_y))[field]
        turned = value.T
        beyond = cols - HALF if field == 0 else HALF - 1
        ex[0, l : l + 1, span(t)] = turned[beyond : beyond + 1]
        et[l, :HALO, span(t)] = turned[:HALO]
        et[l, HALO:, span(t)] = turned[cols - HALO :]

    def put_corners(ct, first, final):
        blank = jnp.zeros((TILE - layers * HALO, cols), F32)
        for n, pieces in enumerate(
            ([value[:HALO] for value in first], [value[TILE - HALO :] for value in final])
        ):
            ct[0, n] = dot(pick[...], jnp.concatenate(pieces + [blank], axis=0).astype(BF16), NT)

    def take_corners(ct, ht):
        for l in range(layers):
            ht[l, :, :TILE] = pltpu.roll(ct[1, 1], TILE - (l + 1) * HALO, axis=1)
            last_tile = ct[1, 0]
            ht[l, :, TILE + rows :] = pltpu.roll(last_tile, TILE - l * HALO, axis=1) if l else last_tile

    def copies(field):
        ext, et, ht, ct, ex = (
            (ext_u, et_u, ht_u, ct_u, ex_u), (ext_y, et_y, ht_y, ct_y, ex_y)
        )[field]
        longer = 1 if field == 0 else -1
        result = []
        for d, (dr, dc) in enumerate(DIRS):
            wide = HALO if dr and dc == longer else MOST
            from_rows = pl.ds(0 if dc < 0 else 2 * HALO - wide, wide)
            to_rows = pl.ds(HALO if dc < 0 else HALO - wide, wide)
            tall = HALO if dr == longer else MOST

            def ends_of(some, t, dr=dr, dc=dc, from_rows=from_rows, to_rows=to_rows, tall=tall):
                if dc == 0:
                    return (
                        y_in.at[some, pl.ds(0 if dr < 0 else rows - tall, tall), :] if t is HBM
                        else ext.at[some, pl.ds(HALO if dr < 0 else HALO + rows - tall, tall), :],
                        ext.at[some, pl.ds(HALO + rows if dr < 0 else HALO - tall, tall), :],
                    )
                if dr == 0:
                    if t is EXTRA:
                        return ex.at[0], ex.at[1]
                    if t is None:
                        return et.at[some, from_rows, :], ht.at[some, to_rows, pl.ds(TILE, rows)]
                    return et.at[some, from_rows, span(t)], ht.at[some, to_rows, span(t, TILE)]
                n = 0 if dr < 0 else 1
                return ct.at[0, n, from_rows, :], ct.at[1, n, to_rows, :]

            def make(some, t=None, d=d, dr=dr, dc=dc, ends_of=ends_of):
                src, dst = ends_of(some, t)
                return pltpu.make_async_remote_copy(
                    src_ref=src, dst_ref=dst, send_sem=send_sem.at[field, d],
                    recv_sem=recv_sem.at[field, d],
                    device_id=(il, ir + dr, ic + dc), device_id_type=MESH,
                )

            to, frm = [], []
            if dr < 0:
                to.append(ir > 0)
                frm.append(ir < nr - 1)
            if dr > 0:
                to.append(ir < nr - 1)
                frm.append(ir > 0)
            if dc < 0:
                to.append(ic > 0)
                frm.append(ic < nc - 1)
            if dc > 0:
                to.append(ic < nc - 1)
                frm.append(ic > 0)

            def both(semaphore, d=d):
                size = above.at[0, pl.ds(0, layers * HALF * rows // cols), :]
                return pltpu.make_async_copy(size, size, semaphore.at[field, d])

            if dr or dc != longer:
                both = None

            result.append(
                (make, both, functools.reduce(jnp.logical_and, to), functools.reduce(jnp.logical_and, frm))
            )
        return result

    halo_copies = (copies(0), copies(1))
    every = slice(None)

    def begin(field, which, some, some_tiles=(None,), whole=False):
        for d in which:
            make, both, to, _ = halo_copies[field][d]

            @pl.when(to)
            def _(make=make, both=both):
                for t in some_tiles:
                    make(some, t).start()
                if whole and both:
                    make(every, EXTRA).start()

    def arrived(field, which):
        for d in which:
            make, both, _, frm = halo_copies[field][d]
            pl.when(frm)(
                lambda make=make, both=both: (both(recv_sem).wait() if both else make(every).wait_recv())
            )

    def departed(field):
        for make, both, to, _ in halo_copies[field]:
            pl.when(to)(
                lambda make=make, both=both: (both(send_sem).wait() if both else make(every).wait_send())
            )

    begin(1, ROWS, every, (HBM,))
    loads[0].wait()
    for t in range(tiles):
        for l in range(layers):
            put_edges(1, l, t, ext_y[l, span(t, HALO), :])
    put_corners(
        ct_y,
        [ext_y[l, span(0, HALO), :] for l in range(layers)],
        [ext_y[l, span(tiles - 1, HALO), :] for l in range(layers)],
    )
    begin(1, SIDE + CORNER, every, whole=True)

    lower, upper = order[::2], order[1::2]

    def portion(t, way):
        if t in (upper, lower)[way]:
            return 0
        return 1 + (lower, upper)[way].index(t) % 2

    def up(step, t):
        side = step % 2
        return pltpu.make_async_remote_copy(
            src_ref=ext_u.at[top, span(t, HALO), :], dst_ref=below.at[side, span(t), :],
            send_sem=zsend.at[side, 0], recv_sem=zrecv.at[side, 0, portion(t, 0)],
            device_id=(il + 1, ir, ic), device_id_type=MESH,
        )

    def down(step, t):
        side = step % 2
        return pltpu.make_async_remote_copy(
            src_ref=ext_u.at[0, span(t, HALO), :], dst_ref=above.at[side, span(t), :],
            send_sem=zsend.at[side, 1], recv_sem=zrecv.at[side, 1, portion(t, 1)],
            device_id=(il - 1, ir, ic), device_id_type=MESH,
        )

    width = layers * 2 * HALO
    for which, start in ((0, -HALF), (1, 1 - HALF)):
        shape = (TILE, TILE + 2 * HALO)
        band_r[which] = window(iota(shape, 1) - HALO - iota(shape, 0), start)
        shape = (TILE, 3 * TILE)
        band_h[which] = window(iota(shape, 1) - TILE - iota(shape, 0), start)
        shape = (cols, cols)
        own_cols = window(iota(shape, 0) - iota(shape, 1), start)
        shape = (2 * HALO, cols)
        k = iota(shape, 0)
        place = jnp.where(k < HALO, k - HALO, k - HALO + cols)
        halo_cols = window(place - iota(shape, 1), start)
        blank = jnp.zeros(shape, BF16)
        for n in range(2):
            inner[which, n * cols : (n + 1) * cols] = own_cols
            for m in range(layers):
                at = n * width + m * 2 * HALO
                for l in range(layers):
                    outer[which, at : at + 2 * HALO, l * cols : (l + 1) * cols] = (
                        halo_cols if m == l else blank
                    )

    def box_own(ext, which, some_tiles):
        pieces = []
        for t in some_tiles:
            tall = pl.ds(t * TILE, TILE + 2 * HALO)
            wide = jnp.concatenate([ext[l, tall, :].astype(BF16) for l in range(layers)], axis=1)
            mid = dot(band_r[which], wide)
            pieces += [
                jnp.concatenate(split(mid[:, l * cols : (l + 1) * cols]), axis=1)
                for l in range(layers)
            ]
        area = dot(jnp.concatenate(pieces, axis=0), inner[which])
        for n, t in enumerate(some_tiles):
            for l in range(layers):
                at = (n * layers + l) * TILE
                part[l, span(t), :] = area[at : at + TILE]

    def box_early(field, which, first=False):
        ext = (ext_u, ext_y)[field]
        if rest:
            box_own(ext, which, rest)
        if first:
            hear(0)
        arrived(field, ROWS)
        if first:
            hear(1)
        box_own(ext, which, ends)
        arrived(field, CORNER + SIDE)
        ht, ex = ((ht_u, ex_u), (ht_y, ex_y))[field]
        take_corners((ct_u, ct_y)[field], ht)
        row = HALO - HALF if field == 0 else HALO + HALF - 1
        for l in range(layers):
            ht[l, row : row + 1, TILE : TILE + rows] = ex[1, l : l + 1]

    def box_late(ht, which, some_tiles):
        halo = jnp.concatenate(
            [ht[:, :, t * TILE : (t + 3) * TILE].reshape(width, 3 * TILE) for t in some_tiles], axis=0
        )
        side = dot(band_h[which], halo.astype(BF16), NT)
        sides = [side[:, n * width : (n + 1) * width] for n in range(len(some_tiles))]
        area = dot(jnp.concatenate([jnp.concatenate(split(v), axis=1) for v in sides], axis=0), outer[which])
        return {
            (l, t): part[l, span(t), :] + area[n * TILE : (n + 1) * TILE, l * cols : (l + 1) * cols]
            for n, t in enumerate(some_tiles)
            for l in range(layers)
        }


    @pl.when(jnp.logical_not(has_above))
    def _():
        z[top] = jnp.zeros((rows, cols), F32)

    for load in loads[2:]:
        load.wait()
    everywhere = [(l, t, (l, span(t), slice(None))) for t in order for l in range(layers)]
    for l, t, at in everywhere:
        level = (capc[at] + 1).astype(F32) * (1.0 / CAP_LEVELS)
        cap[at] = jnp.where(blocked[at] == 1, 0.0, level)

    def fold(value):
        return jnp.sum((value * value).reshape(TILE // 8, 8, cols), axis=0)

    def sums_begin(step, primal_sum, dual_sum):
        left = iota((8, cols), 1) < cols // 2
        both = jnp.where(left, primal_sum, dual_sum)
        across = pltpu.roll(jnp.where(left, dual_sum, primal_sum), cols // 2, axis=1)
        slots[step, pl.ds(me, 1)] = jnp.sum(both + across, axis=0, keepdims=True)[None]

        def send(device):
            pltpu.make_async_remote_copy(
                src_ref=slots.at[step, me], dst_ref=slots.at[step, me],
                send_sem=sum_sem.at[ITERS], recv_sem=sum_sem.at[step],
                device_id=device, device_id_type=MESH,
            ).start()

        ahead(send)

    def sums_end(step, weight):
        some = slots.at[step, pl.ds(0, ndev - 1)]
        pltpu.make_async_copy(some, some, sum_sem.at[step]).wait()
        both = jnp.sum(slots[step], axis=0)
        left = iota((1, cols), 1) < cols // 2
        primal = jnp.sum(jnp.where(left, both, 0.0), axis=1, keepdims=True)
        dual = jnp.sum(jnp.where(left, 0.0, both), axis=1, keepdims=True)
        ratio = jnp.broadcast_to((dual + tiny_term) / (primal + tiny_term), (1, cols))
        return jnp.sqrt(weight) * jnp.sqrt(jnp.sqrt(ratio))

    finish = None
    weight = jnp.ones((1, cols), F32)
    for step in range(ITERS):
        last = step == ITERS - 1
        now = step % 2

        box_early(1, 1, step == 0)
        for (l, t), area in box_late(ht_y, 1, order).items():
            at = (l, span(t), slice(None))
            grad[at] = cost[at] + area * inverse_area
        if step > 0:
            finish(0)
            weight = sums_end(step - 1, weight)
        tau = step_eta / weight
        sigma = step_eta * weight
        sigma_inverse = 1.0 / sigma

        finish_before = finish
        primal_sum = jnp.zeros((8, cols), F32)
        groups = [g for g in (ends, rest) if g]
        if step == 0:
            blocks = [(range(1, layers), g) for g in groups] + [(range(1), [t]) for t in order]
        else:
            blocks = [(range(layers), g) for g in groups]
        for some_layers, some_tiles in blocks:
            if step == 0 and 0 in some_layers:
                for t in some_tiles:
                    pl.when(has_below)(lambda t=t: first_up(t).wait_recv())
            if step > 0 and (some_layers, some_tiles) == blocks[-1]:
                finish_before(1)
            for t in some_tiles:
                for l in some_layers:
                    at = (l, span(t), slice(None))
                    earlier = zlow[span(t), :] if l == 0 else z[l - 1, span(t), :]
                    slope = grad[at] + (z[at] - earlier)
                    old = x[at]
                    new = jnp.minimum(jnp.maximum(old - tau * slope, 0.0), cap[at])
                    moved = new - old
                    x[at] = new
                    primal_sum = primal_sum + fold(moved)
                    value = new + moved + dens[at]
                    ext_u[l, span(t, HALO), :] = value
                    put_edges(0, l, t, value)
            first_layer = some_layers[0]
            some = pl.ds(first_layer, len(some_layers))
            corner_ready = 0 in some_layers and ends[-1] in some_tiles
            if corner_ready:
                put_corners(
                    ct_u,
                    [ext_u[l, span(0, HALO), :] for l in range(layers)],
                    [ext_u[l, span(tiles - 1, HALO), :] for l in range(layers)],
                )
            if 0 in some_layers:

                @pl.when(has_below)
                def _(step=step, some_tiles=some_tiles):
                    for t in some_tiles:
                        if t in lower:
                            down(step, t).start()

            if top in some_layers:
                going = [t for t in some_tiles if t in upper]

                @pl.when(has_above)
                def _(step=step, going=going):
                    for t in going:
                        up(step, t).start()

            begin(0, SIDE, some, some_tiles, (some_layers, some_tiles) == blocks[-1])
            if ends[-1] in some_tiles:
                begin(0, ROWS, some)
            if corner_ready:
                begin(0, CORNER, every)
            if step == 0:
                if (some_layers, some_tiles) == blocks[len(groups)]:
                    hear(2)
        departed(1)
        if step == 0:

            pl.when(has_above)(pltpu.make_async_copy(zlow, zlow, first_sem.at[tiles]).wait)

        dual_sum = jnp.zeros((8, cols), F32)

        def update(old, here, later, keep, sigma=sigma, sigma_inverse=sigma_inverse):
            term = old * sigma_inverse + keep * (here - later)
            return sigma * (term - jnp.clip(term, -layer_gap, layer_gap)) * keep

        for l in range(top):
            for t in order:
                at = (l, span(t), slice(None))
                old = z[at]
                new = update(old, ext_u[l, span(t, HALO), :], ext_u[l + 1, span(t, HALO), :], 1.0)
                z[at] = new
                dual_sum = dual_sum + fold(new - old)

        def other_half(n, last=last, step=step):
            @pl.when(has_below)
            def _():
                for t in upper[n::2]:
                    down(step, t).start()

            if not last:

                @pl.when(has_above)
                def _():
                    for t in lower[n::2]:
                        up(step, t).start()

        box_early(0, 0)
        other_half(0)
        areas = {}
        for t in order:
            if t == ends[0]:
                areas |= box_late(ht_u, 0, ends)
            if rest and t == rest[0]:
                areas |= box_late(ht_u, 0, rest)
            if not last and rest and t == rest[0]:
                put_corners(
                    ct_y,
                    [ext_y[l, span(0, HALO), :] for l in range(layers)],
                    [ext_y[l, span(tiles - 1, HALO), :] for l in range(layers)],
                )
                begin(1, SIDE, every, ends)
                begin(1, ROWS + CORNER, every)
            for l in range(layers):
                area = areas[l, t]
                at = (l, span(t), slice(None))
                old = ext_y[l, span(t, HALO), :]
                term = old * sigma_inverse + area * inverse_area
                capped = jnp.minimum(term, high_density)
                clipped = jnp.where(blocked[at] == 0, jnp.maximum(capped, low_density), capped)
                new = sigma * (term - clipped)
                dual_sum = dual_sum + fold(new - old)
                if last:
                    y_out[at] = new
                else:
                    ext_y[l, span(t, HALO), :] = new
                    put_edges(1, l, t, new)

        if not last:
            begin(1, SIDE, every, rest, True)

        def update_top(t, now=now, update=update):
            at = (top, span(t), slice(None))
            old = z[at]
            new = update(old, ext_u[top, span(t, HALO), :], above[now, span(t), :], keep_top)
            z[at] = new
            return fold(new - old)

        def update_low(t, now=now, update=update):
            old = zlow[span(t), :]
            new = update(old, below[now, span(t), :], ext_u[0, span(t, HALO), :], keep_low)
            zlow[span(t), :] = new
            return fold(new - old)

        def landed(downs, ups, now=now):
            for there, plane, way, some in (
                (has_above, above, 1, downs), (has_below, below, 0, ups)
            ):
                if some:
                    all_of = plane.at[now, pl.ds(0, len(some) * TILE), :]
                    which = portion(some[0], way)
                    pl.when(there)(
                        pltpu.make_async_copy(all_of, all_of, zrecv.at[now, way, which]).wait
                    )

        landed(lower, upper)
        for t in lower:
            dual_sum = dual_sum + update_top(t)
        for t in upper:
            dual_sum = dual_sum + update_low(t)
        if step == 0:
            for n in range(3, rounds):
                hear(n)
        sums_begin(step, primal_sum, dual_sum)
        other_half(1)

        def finish(n, last=last, step=step, now=now, landed=landed,
                   update_top=update_top, update_low=update_low):
            if n == 0:
                for there, way, gone in (
                    (has_below, 1, order), (has_above, 0, upper if last else order)
                ):
                    all_of = above.at[now, pl.ds(0, len(gone) * TILE), :]
                    pl.when(there)(pltpu.make_async_copy(all_of, all_of, zsend.at[now, way]).wait)
                departed(0)
            landed(upper[n::2], [] if last else lower[n::2])
            for t in upper[n::2]:
                update_top(t)
            if not last:
                for t in lower[n::2]:
                    update_low(t)

    finish(0)
    finish(1)
    weight_out[...] = sums_end(ITERS - 1, weight)
    gone = slots.at[:, pl.ds(0, ndev - 1)]
    pltpu.make_async_copy(gone, gone, sum_sem.at[ITERS]).wait()


def flush(*refs):
    count = len(refs) // 2
    ins, outs, sem = refs[:count], refs[count : 2 * count], refs[2 * count]
    moves = [
        pltpu.make_async_copy(a.at[l, some], b.at[l, some], sem.at[n])
        for n, (a, b) in enumerate(zip(ins, outs))
        for l in range(a.shape[0])
        for some in (pl.ds(0, a.shape[1] // 2), pl.ds(a.shape[1] // 2, a.shape[1] // 2))
    ]
    for move in moves:
        move.start()
    for n, (a, b) in enumerate(zip(ins, outs)):
        pltpu.make_async_copy(a, b, sem.at[n]).wait()


def local(sizes, *args):
    layers, rows, cols = args[0].shape
    ndev = sizes[0] * sizes[1] * sizes[2]
    tiles = rows // TILE
    vmem = pl.BlockSpec(memory_space=pltpu.VMEM)
    anywhere = pl.BlockSpec(memory_space=pl.ANY)
    full = pltpu.VMEM((layers, rows, cols), F32)
    fields = pltpu.VMEM((2, layers, rows, cols), F32)
    field_flags = pltpu.VMEM((2, layers, rows, cols), jnp.int32)
    line = pltpu.VMEM((1, cols), F32)
    ext = pltpu.VMEM((layers, rows + 2 * HALO, cols), F32)
    et = pltpu.VMEM((layers, 2 * HALO, rows), F32)
    ht = pltpu.VMEM((layers, 2 * HALO, rows + 2 * TILE), F32)
    ct = pltpu.VMEM((2, 2, 2 * HALO, TILE), F32)
    ex = pltpu.VMEM((2, layers, rows), F32)
    plane = pltpu.VMEM((rows, cols), F32)
    planes = pltpu.VMEM((2, rows, cols), F32)
    x, y, z, weight = pl.pallas_call(
        functools.partial(kernel, sizes),
        out_shape=(full, full, full, line),
        in_specs=[anywhere] * 7,
        out_specs=(vmem,) * 4,
        scratch_shapes=[
            fields, field_flags,
            ext, ext, et, et, ht, ht, ct, ct, ex, ex, planes, planes, plane, full, full, full,
            pltpu.VMEM((2, TILE, TILE + 2 * HALO), BF16),
            pltpu.VMEM((2, TILE, 3 * TILE), BF16),
            pltpu.VMEM((2, 2 * cols, cols), BF16),
            pltpu.VMEM((2, 2 * layers * 2 * HALO, layers * cols), BF16),
            pltpu.VMEM((2 * HALO, cols), BF16),
            pltpu.VMEM((ITERS, ndev, 1, cols), F32),
            pltpu.SemaphoreType.DMA((5,)),
            pltpu.SemaphoreType.DMA((2, 8)),
            pltpu.SemaphoreType.DMA((2, 8)),
            pltpu.SemaphoreType.DMA((tiles + 1,)),
            pltpu.SemaphoreType.DMA((2, 2)),
            pltpu.SemaphoreType.DMA((2, 2, 3)),
            pltpu.SemaphoreType.DMA((ITERS + 1,)),
            pltpu.SemaphoreType.REGULAR((len(spreads(sizes)) + 2,)),
        ],
        compiler_params=pltpu.CompilerParams(collective_id=0, has_side_effects=True),
        name="fill_steps",
    )(*args)
    whole = jax.ShapeDtypeStruct((layers, rows, cols), F32)
    x, y, z = pl.pallas_call(
        flush,
        out_shape=(whole,) * 3,
        in_specs=[anywhere] * 3,
        out_specs=(anywhere,) * 3,
        scratch_shapes=[pltpu.SemaphoreType.DMA((3,))],
        name="flush",
    )(*(pltpu.with_memory_space_constraint(value, pltpu.VMEM) for value in (x, y, z)))
    return x, y, z, weight[0, 0]


def solution(mesh):
    sizes = tuple(mesh.shape[axis] for axis in ("layer", "row", "col"))
    spec = P("layer", "row", "col")
    return jax.shard_map(
        functools.partial(local, sizes),
        mesh=mesh,
        in_specs=(spec,) * 7,
        out_specs=(spec, spec, spec, P()),
        check_vma=False,
    )
```

```python
import functools

import jax
import jax.numpy as jnp
from jax import lax
from jax.experimental import pallas as pl
from jax.experimental.pallas import tpu as pltpu
from jax.sharding import PartitionSpec as P

WIN = 50
CAP_LEVELS = 8
ITERS = 3

step_eta = 0.4
low_density = 0.35
high_density = 0.65
layer_gap = 0.15
tiny_term = 1e-06

HALF = WIN // 2
HALO = -(-HALF // 16) * 16
MOST = (HALF - 1) // 8 * 8
assert WIN == 2 * HALF and MOST == HALF - 1
TILE = 128
MESH = pl.DeviceIdType.MESH
HBM, EXTRA = "hbm", "extra"
DIRS = ((-1, 0), (1, 0), (0, -1), (0, 1), (-1, -1), (-1, 1), (1, -1), (1, 1))
ROWS = (0, 1)
SIDE = (2, 3)
CORNER = (4, 5, 6, 7)
F32 = jnp.float32
BF16 = jnp.bfloat16
NT = (((1,), (1,)), ((), ()))
NN = (((1,), (0,)), ((), ()))


def split(value):
    high = value.astype(BF16)
    low = (value - high.astype(F32)).astype(BF16)
    return high, low


def dot(left, right, dims=NN):
    return lax.dot_general(left, right, dims, preferred_element_type=F32)


def iota(shape, dim):
    return lax.broadcasted_iota(jnp.int32, shape, dim)


def window(offset, start):
    return jnp.where((offset >= start) & (offset < start + WIN), 1.0, 0.0).astype(BF16)


def spreads(sizes):
    distance, result = 1, []
    while distance < max(sizes) - 1:
        result.append(distance)
        distance *= 2
    return result


def kernel(
    sizes, cost_in, dens_in, capc_in, blocked_in, x_in, y_in, z_in,
    x, y_out, z, weight_out,
    reals, flags,
    ext_u, ext_y, et_u, et_y, ht_u, ht_y, ct_u, ct_y, ex_u, ex_y, above, below, zlow, cap, grad, part,
    band_r, band_h, inner, outer, pick, slots,
    load_sem, send_sem, recv_sem, first_sem, zsend, zrecv, sum_sem, ready,
):
    nl, nr, nc = sizes
    layers, rows, cols = x_in.shape
    top = layers - 1
    ndev = nl * nr * nc
    il, ir, ic = lax.axis_index("layer"), lax.axis_index("row"), lax.axis_index("col")
    me = (il * nr + ir) * nc + ic
    cost, dens, capc, blocked = reals.at[0], reals.at[1], flags.at[0], flags.at[1]
    tiles = rows // TILE
    order = list(dict.fromkeys((0, tiles - 1, *range(tiles))))
    ends = order[:2]
    rest = order[2:]
    inverse_area = 1.0 / (WIN * WIN)
    own = pl.ds(HALO, rows)
    has_above, has_below = il < nl - 1, il > 0

    pairs = (
        (y_in, ext_y.at[:, own, :], 0), (z_in, z, 1), (cost_in, cost, 2), (dens_in, dens, 2),
        (x_in, x, 3), (capc_in, capc, 4), (blocked_in, blocked, 4),
    )
    loads = [
        pltpu.make_async_copy(ref, ref, load_sem.at[n])
        for n, ref in enumerate((ext_y.at[:, own, :], z, reals, x, flags))
    ]

    for ref in (ext_u, ext_y):
        ref[:, :HALO, :] = jnp.zeros((layers, HALO, cols), F32)
        ref[:, HALO + rows :, :] = jnp.zeros((layers, HALO, cols), F32)
    for ref in (ht_u, ht_y, ct_u, ct_y, ex_u, ex_y):
        ref[...] = jnp.zeros(ref.shape, F32)

    barrier = pltpu.get_barrier_semaphore()

    def ahead(act):
        def one(k, _):
            i = lax.rem(me + k, ndev)
            act((i // (nr * nc), (i // nc) % nr, i % nc))
            return 0

        lax.fori_loop(1, ndev, one, 0, unroll=ndev <= 32)

    def lines(act):
        for n in range(1, nl):
            act((lax.rem(il + n, nl), ir, ic))
        for n in range(1, nr):
            act((il, lax.rem(ir + n, nr), ic))
        for n in range(1, nc):
            act((il, ir, lax.rem(ic + n, nc)))

    def beside(distance):
        peers = []
        for axis, (at, n) in enumerate(((il, nl), (ir, nr), (ic, nc))):
            if distance < n:
                for there, to in ((at >= distance, at - distance), (at < n - distance, at + distance)):
                    device = [il, ir, ic]
                    device[axis] = to
                    peers.append((there, tuple(device)))
        return peers

    line_peers = nl + nr + nc - 3
    corners = []
    for dr, dc in DIRS[4:]:
        there = jnp.logical_and(
            ir < nr - 1 if dr > 0 else ir > 0, ic < nc - 1 if dc > 0 else ic > 0
        )
        corners.append((there, (il, ir + dr, ic + dc)))

    def signal(semaphore, device):
        pl.semaphore_signal(semaphore, inc=1, device_id=device, device_id_type=MESH)

    def signal_some(semaphore, peers):
        for there, device in peers:
            pl.when(there)(functools.partial(signal, semaphore, device))

    def wait_some(semaphore, peers):
        pl.semaphore_wait(semaphore, sum(there.astype(jnp.int32) for there, _ in peers))

    signal_some(barrier, beside(1) + corners)
    for a, b, n in pairs:
        pltpu.make_async_copy(a, b, load_sem.at[n]).start()

    @pl.when(jnp.logical_not(has_above))
    def _():
        above[...] = jnp.zeros(above.shape, F32)

    @pl.when(jnp.logical_not(has_below))
    def _():
        below[...] = jnp.zeros(below.shape, F32)
        zlow[...] = jnp.zeros(zlow.shape, F32)

    spread = spreads(sizes)
    rounds = len(spread) + 2

    def tell(n):
        if n < len(spread):
            signal_some(ready.at[n], beside(spread[n]))
        elif n < rounds:
            lines(functools.partial(signal, ready.at[n]))

    def hear(n):
        if n < len(spread):
            wait_some(ready.at[n], beside(spread[n]))
        elif n < rounds:
            pl.semaphore_wait(ready.at[n], line_peers)
        tell(n + 1)

    def span(t, base=0):
        return pl.ds(t * TILE + base, TILE)

    wait_some(barrier, beside(1) + corners)

    def first_up(t):
        return pltpu.make_async_remote_copy(
            src_ref=z.at[top, span(t), :], dst_ref=zlow.at[span(t), :],
            send_sem=first_sem.at[tiles], recv_sem=first_sem.at[t],
            device_id=(il + 1, ir, ic), device_id_type=MESH,
        )

    loads[1].wait()

    @pl.when(has_above)
    def _():
        for t in order:
            first_up(t).start()


    tell(0)

    keep_top = jnp.where(has_above, 1.0, 0.0).astype(F32)
    keep_low = jnp.where(has_below, 1.0, 0.0).astype(F32)
    shape = (2 * HALO, cols)
    k = iota(shape, 0)
    place = jnp.where(k < HALO, k, k - 2 * HALO + cols)
    pick[...] = jnp.where(place == iota(shape, 1), 1.0, 0.0).astype(BF16)

    def put_edges(field, l, t, value):
        et, ex = ((et_u, ex_u), (et_y, ex_y))[field]
        turned = value.T
        beyond = cols - HALF if field == 0 else HALF - 1
        ex[0, l : l + 1, span(t)] = turned[beyond : beyond + 1]
        et[l, :HALO, span(t)] = turned[:HALO]
        et[l, HALO:, span(t)] = turned[cols - HALO :]

    def put_corners(ct, first, final):
        blank = jnp.zeros((TILE - layers * HALO, cols), F32)
        for n, pieces in enumerate(
            ([value[:HALO] for value in first], [value[TILE - HALO :] for value in final])
        ):
            ct[0, n] = dot(pick[...], jnp.concatenate(pieces + [blank], axis=0).astype(BF16), NT)

    def take_corners(ct, ht):
        for l in range(layers):
            ht[l, :, :TILE] = pltpu.roll(ct[1, 1], TILE - (l + 1) * HALO, axis=1)
            last_tile = ct[1, 0]
            ht[l, :, TILE + rows :] = pltpu.roll(last_tile, TILE - l * HALO, axis=1) if l else last_tile

    def copies(field):
        ext, et, ht, ct, ex = (
            (ext_u, et_u, ht_u, ct_u, ex_u), (ext_y, et_y, ht_y, ct_y, ex_y)
        )[field]
        longer = 1 if field == 0 else -1
        result = []
        for d, (dr, dc) in enumerate(DIRS):
            wide = HALO if dr and dc == longer else MOST
            from_rows = pl.ds(0 if dc < 0 else 2 * HALO - wide, wide)
            to_rows = pl.ds(HALO if dc < 0 else HALO - wide, wide)
            tall = HALO if dr == longer else MOST

            def ends_of(some, t, dr=dr, dc=dc, from_rows=from_rows, to_rows=to_rows, tall=tall):
                if dc == 0:
                    return (
                        y_in.at[some, pl.ds(0 if dr < 0 else rows - tall, tall), :] if t is HBM
                        else ext.at[some, pl.ds(HALO if dr < 0 else HALO + rows - tall, tall), :],
                        ext.at[some, pl.ds(HALO + rows if dr < 0 else HALO - tall, tall), :],
                    )
                if dr == 0:
                    if t is EXTRA:
                        return ex.at[0], ex.at[1]
                    if t is None:
                        return et.at[some, from_rows, :], ht.at[some, to_rows, pl.ds(TILE, rows)]
                    return et.at[some, from_rows, span(t)], ht.at[some, to_rows, span(t, TILE)]
                n = 0 if dr < 0 else 1
                return ct.at[0, n, from_rows, :], ct.at[1, n, to_rows, :]

            def make(some, t=None, d=d, dr=dr, dc=dc, ends_of=ends_of):
                src, dst = ends_of(some, t)
                return pltpu.make_async_remote_copy(
                    src_ref=src, dst_ref=dst, send_sem=send_sem.at[field, d],
                    recv_sem=recv_sem.at[field, d],
                    device_id=(il, ir + dr, ic + dc), device_id_type=MESH,
                )

            to, frm = [], []
            if dr < 0:
                to.append(ir > 0)
                frm.append(ir < nr - 1)
            if dr > 0:
                to.append(ir < nr - 1)
                frm.append(ir > 0)
            if dc < 0:
                to.append(ic > 0)
                frm.append(ic < nc - 1)
            if dc > 0:
                to.append(ic < nc - 1)
                frm.append(ic > 0)

            def both(semaphore, d=d):
                size = above.at[0, pl.ds(0, layers * HALF * rows // cols), :]
                return pltpu.make_async_copy(size, size, semaphore.at[field, d])

            if dr or dc != longer:
                both = None

            result.append(
                (make, both, functools.reduce(jnp.logical_and, to), functools.reduce(jnp.logical_and, frm))
            )
        return result

    halo_copies = (copies(0), copies(1))
    every = slice(None)

    def begin(field, which, some, some_tiles=(None,), whole=False):
        for d in which:
            make, both, to, _ = halo_copies[field][d]

            @pl.when(to)
            def _(make=make, both=both):
                for t in some_tiles:
                    make(some, t).start()
                if whole and both:
                    make(every, EXTRA).start()

    def arrived(field, which):
        for d in which:
            make, both, _, frm = halo_copies[field][d]
            pl.when(frm)(
                lambda make=make, both=both: (both(recv_sem).wait() if both else make(every).wait_recv())
            )

    def departed(field):
        for make, both, to, _ in halo_copies[field]:
            pl.when(to)(
                lambda make=make, both=both: (both(send_sem).wait() if both else make(every).wait_send())
            )

    begin(1, ROWS, every, (HBM,))
    loads[0].wait()
    for t in range(tiles):
        for l in range(layers):
            put_edges(1, l, t, ext_y[l, span(t, HALO), :])
    put_corners(
        ct_y,
        [ext_y[l, span(0, HALO), :] for l in range(layers)],
        [ext_y[l, span(tiles - 1, HALO), :] for l in range(layers)],
    )
    begin(1, SIDE + CORNER, every, whole=True)

    lower, upper = order[::2], order[1::2]

    def portion(t, way):
        if t in (upper, lower)[way]:
            return 0
        return 1 + (lower, upper)[way].index(t) % 2

    def up(step, t):
        side = step % 2
        return pltpu.make_async_remote_copy(
            src_ref=ext_u.at[top, span(t, HALO), :], dst_ref=below.at[side, span(t), :],
            send_sem=zsend.at[side, 0], recv_sem=zrecv.at[side, 0, portion(t, 0)],
            device_id=(il + 1, ir, ic), device_id_type=MESH,
        )

    def down(step, t):
        side = step % 2
        return pltpu.make_async_remote_copy(
            src_ref=ext_u.at[0, span(t, HALO), :], dst_ref=above.at[side, span(t), :],
            send_sem=zsend.at[side, 1], recv_sem=zrecv.at[side, 1, portion(t, 1)],
            device_id=(il - 1, ir, ic), device_id_type=MESH,
        )

    width = layers * 2 * HALO
    for which, start in ((0, -HALF), (1, 1 - HALF)):
        shape = (TILE, TILE + 2 * HALO)
        band_r[which] = window(iota(shape, 1) - HALO - iota(shape, 0), start)
        shape = (TILE, 3 * TILE)
        band_h[which] = window(iota(shape, 1) - TILE - iota(shape, 0), start)
        shape = (cols, cols)
        own_cols = window(iota(shape, 0) - iota(shape, 1), start)
        shape = (2 * HALO, cols)
        k = iota(shape, 0)
        place = jnp.where(k < HALO, k - HALO, k - HALO + cols)
        halo_cols = window(place - iota(shape, 1), start)
        blank = jnp.zeros(shape, BF16)
        for n in range(2):
            inner[which, n * cols : (n + 1) * cols] = own_cols
            for m in range(layers):
                at = n * width + m * 2 * HALO
                for l in range(layers):
                    outer[which, at : at + 2 * HALO, l * cols : (l + 1) * cols] = (
                        halo_cols if m == l else blank
                    )

    def box_own(ext, which, some_tiles):
        pieces = []
        for t in some_tiles:
            tall = pl.ds(t * TILE, TILE + 2 * HALO)
            wide = jnp.concatenate([ext[l, tall, :].astype(BF16) for l in range(layers)], axis=1)
            mid = dot(band_r[which], wide)
            pieces += [
                jnp.concatenate(split(mid[:, l * cols : (l + 1) * cols]), axis=1)
                for l in range(layers)
            ]
        area = dot(jnp.concatenate(pieces, axis=0), inner[which])
        for n, t in enumerate(some_tiles):
            for l in range(layers):
                at = (n * layers + l) * TILE
                part[l, span(t), :] = area[at : at + TILE]

    def box_early(field, which, first=False):
        ext = (ext_u, ext_y)[field]
        if rest:
            box_own(ext, which, rest)
        if first:
            hear(0)
        arrived(field, ROWS)
        if first:
            hear(1)
        box_own(ext, which, ends)
        arrived(field, CORNER + SIDE)
        ht, ex = ((ht_u, ex_u), (ht_y, ex_y))[field]
        take_corners((ct_u, ct_y)[field], ht)
        row = HALO - HALF if field == 0 else HALO + HALF - 1
        for l in range(layers):
            ht[l, row : row + 1, TILE : TILE + rows] = ex[1, l : l + 1]

    def box_late(ht, which, some_tiles):
        halo = jnp.concatenate(
            [ht[:, :, t * TILE : (t + 3) * TILE].reshape(width, 3 * TILE) for t in some_tiles], axis=0
        )
        side = dot(band_h[which], halo.astype(BF16), NT)
        sides = [side[:, n * width : (n + 1) * width] for n in range(len(some_tiles))]
        area = dot(jnp.concatenate([jnp.concatenate(split(v), axis=1) for v in sides], axis=0), outer[which])
        return {
            (l, t): part[l, span(t), :] + area[n * TILE : (n + 1) * TILE, l * cols : (l + 1) * cols]
            for n, t in enumerate(some_tiles)
            for l in range(layers)
        }


    @pl.when(jnp.logical_not(has_above))
    def _():
        z[top] = jnp.zeros((rows, cols), F32)

    for load in loads[2:]:
        load.wait()
    everywhere = [(l, t, (l, span(t), slice(None))) for t in order for l in range(layers)]
    for l, t, at in everywhere:
        level = (capc[at] + 1).astype(F32) * (1.0 / CAP_LEVELS)
        cap[at] = jnp.where(blocked[at] == 1, 0.0, level)

    def fold(value):
        return jnp.sum((value * value).reshape(TILE // 8, 8, cols), axis=0)

    def sums_begin(step, primal_sum, dual_sum):
        left = iota((8, cols), 1) < cols // 2
        both = jnp.where(left, primal_sum, dual_sum)
        across = pltpu.roll(jnp.where(left, dual_sum, primal_sum), cols // 2, axis=1)
        slots[step, pl.ds(me, 1)] = jnp.sum(both + across, axis=0, keepdims=True)[None]

        def send(device):
            pltpu.make_async_remote_copy(
                src_ref=slots.at[step, me], dst_ref=slots.at[step, me],
                send_sem=sum_sem.at[ITERS], recv_sem=sum_sem.at[step],
                device_id=device, device_id_type=MESH,
            ).start()

        ahead(send)

    def sums_end(step, weight):
        some = slots.at[step, pl.ds(0, ndev - 1)]
        pltpu.make_async_copy(some, some, sum_sem.at[step]).wait()
        both = jnp.sum(slots[step], axis=0)
        left = iota((1, cols), 1) < cols // 2
        primal = jnp.sum(jnp.where(left, both, 0.0), axis=1, keepdims=True)
        dual = jnp.sum(jnp.where(left, 0.0, both), axis=1, keepdims=True)
        ratio = jnp.broadcast_to((dual + tiny_term) / (primal + tiny_term), (1, cols))
        return jnp.sqrt(weight) * jnp.sqrt(jnp.sqrt(ratio))

    finish = None
    weight = jnp.ones((1, cols), F32)
    for step in range(ITERS):
        last = step == ITERS - 1
        now = step % 2

        box_early(1, 1, step == 0)
        for (l, t), area in box_late(ht_y, 1, order).items():
            at = (l, span(t), slice(None))
            grad[at] = cost[at] + area * inverse_area
        if step > 0:
            finish(0)
            weight = sums_end(step - 1, weight)
        tau = step_eta / weight
        sigma = step_eta * weight
        sigma_inverse = 1.0 / sigma

        finish_before = finish
        primal_sum = jnp.zeros((8, cols), F32)
        groups = [g for g in (ends, rest) if g]
        if step == 0:
            blocks = [(range(1, layers), g) for g in groups] + [(range(1), [t]) for t in order]
        else:
            blocks = [(range(layers), g) for g in groups]
        for some_layers, some_tiles in blocks:
            if step == 0 and 0 in some_layers:
                for t in some_tiles:
                    pl.when(has_below)(lambda t=t: first_up(t).wait_recv())
            if step > 0 and (some_layers, some_tiles) == blocks[-1]:
                finish_before(1)
            for t in some_tiles:
                for l in some_layers:
                    at = (l, span(t), slice(None))
                    earlier = zlow[span(t), :] if l == 0 else z[l - 1, span(t), :]
                    slope = grad[at] + (z[at] - earlier)
                    old = x[at]
                    new = jnp.minimum(jnp.maximum(old - tau * slope, 0.0), cap[at])
                    moved = new - old
                    x[at] = new
                    primal_sum = primal_sum + fold(moved)
                    value = new + moved + dens[at]
                    ext_u[l, span(t, HALO), :] = value
                    put_edges(0, l, t, value)
            first_layer = some_layers[0]
            some = pl.ds(first_layer, len(some_layers))
            corner_ready = 0 in some_layers and ends[-1] in some_tiles
            if corner_ready:
                put_corners(
                    ct_u,
                    [ext_u[l, span(0, HALO), :] for l in range(layers)],
                    [ext_u[l, span(tiles - 1, HALO), :] for l in range(layers)],
                )
            if 0 in some_layers:

                @pl.when(has_below)
                def _(step=step, some_tiles=some_tiles):
                    for t in some_tiles:
                        if t in lower:
                            down(step, t).start()

            if top in some_layers:
                going = [t for t in some_tiles if t in upper]

                @pl.when(has_above)
                def _(step=step, going=going):
                    for t in going:
                        up(step, t).start()

            begin(0, SIDE, some, some_tiles, (some_layers, some_tiles) == blocks[-1])
            if ends[-1] in some_tiles:
                begin(0, ROWS, some)
            if corner_ready:
                begin(0, CORNER, every)
            if step == 0:
                if (some_layers, some_tiles) == blocks[len(groups)]:
                    hear(2)
        departed(1)
        if step == 0:

            pl.when(has_above)(pltpu.make_async_copy(zlow, zlow, first_sem.at[tiles]).wait)

        dual_sum = jnp.zeros((8, cols), F32)

        def update(old, here, later, keep, sigma=sigma, sigma_inverse=sigma_inverse):
            term = old * sigma_inverse + keep * (here - later)
            return sigma * (term - jnp.clip(term, -layer_gap, layer_gap)) * keep

        for l in range(top):
            for t in order:
                at = (l, span(t), slice(None))
                old = z[at]
                new = update(old, ext_u[l, span(t, HALO), :], ext_u[l + 1, span(t, HALO), :], 1.0)
                z[at] = new
                dual_sum = dual_sum + fold(new - old)

        def other_half(n, last=last, step=step):
            @pl.when(has_below)
            def _():
                for t in upper[n::2]:
                    down(step, t).start()

            if not last:

                @pl.when(has_above)
                def _():
                    for t in lower[n::2]:
                        up(step, t).start()

        box_early(0, 0)
        if not last:
            other_half(0)
        areas = {}
        for t in order:
            if t == ends[0]:
                areas |= box_late(ht_u, 0, ends)
            if rest and t == rest[0]:
                areas |= box_late(ht_u, 0, rest)
            if not last and rest and t == rest[0]:
                put_corners(
                    ct_y,
                    [ext_y[l, span(0, HALO), :] for l in range(layers)],
                    [ext_y[l, span(tiles - 1, HALO), :] for l in range(layers)],
                )
                begin(1, SIDE, every, ends)
                begin(1, ROWS + CORNER, every)
            for l in range(layers):
                area = areas[l, t]
                at = (l, span(t), slice(None))
                old = ext_y[l, span(t, HALO), :]
                term = old * sigma_inverse + area * inverse_area
                capped = jnp.minimum(term, high_density)
                clipped = jnp.where(blocked[at] == 0, jnp.maximum(capped, low_density), capped)
                new = sigma * (term - clipped)
                dual_sum = dual_sum + fold(new - old)
                if last:
                    y_out[at] = new
                else:
                    ext_y[l, span(t, HALO), :] = new
                    put_edges(1, l, t, new)

        if not last:
            begin(1, SIDE, every, rest, True)

        def update_top(t, now=now, update=update):
            at = (top, span(t), slice(None))
            old = z[at]
            new = update(old, ext_u[top, span(t, HALO), :], above[now, span(t), :], keep_top)
            z[at] = new
            return fold(new - old)

        def update_low(t, now=now, update=update):
            old = zlow[span(t), :]
            new = update(old, below[now, span(t), :], ext_u[0, span(t, HALO), :], keep_low)
            zlow[span(t), :] = new
            return fold(new - old)

        def landed(downs, ups, now=now):
            for there, plane, way, some in (
                (has_above, above, 1, downs), (has_below, below, 0, ups)
            ):
                if some:
                    all_of = plane.at[now, pl.ds(0, len(some) * TILE), :]
                    which = portion(some[0], way)
                    pl.when(there)(
                        pltpu.make_async_copy(all_of, all_of, zrecv.at[now, way, which]).wait
                    )

        landed(lower, upper)
        for t in lower:
            dual_sum = dual_sum + update_top(t)
        for t in upper:
            dual_sum = dual_sum + update_low(t)
        if step == 0:
            for n in range(3, rounds):
                hear(n)
        sums_begin(step, primal_sum, dual_sum)
        if last:
            other_half(0)
        other_half(1)

        def finish(n, last=last, step=step, now=now, landed=landed,
                   update_top=update_top, update_low=update_low):
            if n == 0:
                for there, way, gone in (
                    (has_below, 1, order), (has_above, 0, upper if last else order)
                ):
                    all_of = above.at[now, pl.ds(0, len(gone) * TILE), :]
                    pl.when(there)(pltpu.make_async_copy(all_of, all_of, zsend.at[now, way]).wait)
                departed(0)
            landed(upper[n::2], [] if last else lower[n::2])
            for t in upper[n::2]:
                update_top(t)
            if not last:
                for t in lower[n::2]:
                    update_low(t)

    finish(0)
    finish(1)
    weight_out[...] = sums_end(ITERS - 1, weight)
    gone = slots.at[:, pl.ds(0, ndev - 1)]
    pltpu.make_async_copy(gone, gone, sum_sem.at[ITERS]).wait()


def flush(*refs):
    count = len(refs) // 2
    ins, outs, sem = refs[:count], refs[count : 2 * count], refs[2 * count]
    moves = [
        pltpu.make_async_copy(a.at[l, some], b.at[l, some], sem.at[n])
        for n, (a, b) in enumerate(zip(ins, outs))
        for l in range(a.shape[0])
        for some in (pl.ds(0, a.shape[1] // 2), pl.ds(a.shape[1] // 2, a.shape[1] // 2))
    ]
    for move in moves:
        move.start()
    for n, (a, b) in enumerate(zip(ins, outs)):
        pltpu.make_async_copy(a, b, sem.at[n]).wait()


def local(sizes, *args):
    layers, rows, cols = args[0].shape
    ndev = sizes[0] * sizes[1] * sizes[2]
    tiles = rows // TILE
    vmem = pl.BlockSpec(memory_space=pltpu.VMEM)
    anywhere = pl.BlockSpec(memory_space=pl.ANY)
    full = pltpu.VMEM((layers, rows, cols), F32)
    fields = pltpu.VMEM((2, layers, rows, cols), F32)
    field_flags = pltpu.VMEM((2, layers, rows, cols), jnp.int32)
    line = pltpu.VMEM((1, cols), F32)
    ext = pltpu.VMEM((layers, rows + 2 * HALO, cols), F32)
    et = pltpu.VMEM((layers, 2 * HALO, rows), F32)
    ht = pltpu.VMEM((layers, 2 * HALO, rows + 2 * TILE), F32)
    ct = pltpu.VMEM((2, 2, 2 * HALO, TILE), F32)
    ex = pltpu.VMEM((2, layers, rows), F32)
    plane = pltpu.VMEM((rows, cols), F32)
    planes = pltpu.VMEM((2, rows, cols), F32)
    x, y, z, weight = pl.pallas_call(
        functools.partial(kernel, sizes),
        out_shape=(full, full, full, line),
        in_specs=[anywhere] * 7,
        out_specs=(vmem,) * 4,
        scratch_shapes=[
            fields, field_flags,
            ext, ext, et, et, ht, ht, ct, ct, ex, ex, planes, planes, plane, full, full, full,
            pltpu.VMEM((2, TILE, TILE + 2 * HALO), BF16),
            pltpu.VMEM((2, TILE, 3 * TILE), BF16),
            pltpu.VMEM((2, 2 * cols, cols), BF16),
            pltpu.VMEM((2, 2 * layers * 2 * HALO, layers * cols), BF16),
            pltpu.VMEM((2 * HALO, cols), BF16),
            pltpu.VMEM((ITERS, ndev, 1, cols), F32),
            pltpu.SemaphoreType.DMA((5,)),
            pltpu.SemaphoreType.DMA((2, 8)),
            pltpu.SemaphoreType.DMA((2, 8)),
            pltpu.SemaphoreType.DMA((tiles + 1,)),
            pltpu.SemaphoreType.DMA((2, 2)),
            pltpu.SemaphoreType.DMA((2, 2, 3)),
            pltpu.SemaphoreType.DMA((ITERS + 1,)),
            pltpu.SemaphoreType.REGULAR((len(spreads(sizes)) + 2,)),
        ],
        compiler_params=pltpu.CompilerParams(collective_id=0, has_side_effects=True),
        name="fill_steps",
    )(*args)
    whole = jax.ShapeDtypeStruct((layers, rows, cols), F32)
    x, y, z = pl.pallas_call(
        flush,
        out_shape=(whole,) * 3,
        in_specs=[anywhere] * 3,
        out_specs=(anywhere,) * 3,
        scratch_shapes=[pltpu.SemaphoreType.DMA((3,))],
        name="flush",
    )(*(pltpu.with_memory_space_constraint(value, pltpu.VMEM) for value in (x, y, z)))
    return x, y, z, weight[0, 0]


def solution(mesh):
    sizes = tuple(mesh.shape[axis] for axis in ("layer", "row", "col"))
    spec = P("layer", "row", "col")
    return jax.shard_map(
        functools.partial(local, sizes),
        mesh=mesh,
        in_specs=(spec,) * 7,
        out_specs=(spec, spec, spec, P()),
        check_vma=False,
    )
```
